128 devices in a mesh: hx: 8 (over y, core), hy: 16 (over x, z).
Axes of the slice: x: 4, y: 4, z: 4, core: 2. Of those that a mesh axis runs over, the one named last changes fastest.
Arguments:
- embeddings: bfloat16 [65536, 768], P(('hx', 'hy')), may hold values from -60 to 60
- bucket: int32 [65536], P(('hx', 'hy')), may hold values from 0 to 255, as said below
Outputs:
- smoothed: bfloat16 [65536, 768], P(('hx', 'hy'))
The draws below stay inside these ranges and needn't reach their ends.
Inputs may be any that keep to these rules, and one draw needn't show every extreme that they name: Every bucket holds at most 512 files and some bucket holds exactly 512; buckets may be empty. The files of each bucket, and of each owner's 2 buckets taken together, lie on the devices as evenly as can be (counts on two devices differ by at most one), so that no device holds more than 8 files of one owner's buckets, and some owner's buckets give exactly 8 to every device.
All inputs are finite; a program needn't handle non-finite values.
Results may differ from the reference program's by a relative error of at most 0.0042.
Values may be sent and summed in bfloat16 or wider, within the bound.
A program may use at most 64 MiB of HBM per device.

```python
import math
import jax
import jax.numpy as jnp
from jax import lax

D = 768
BPD = 2
F_DEV = 512
CAP = 512
FILES = 65536
N_HX = 8
N_HY = 16


def draw_bucket(key, part):
    devices_all = N_HX * N_HY
    bucket_total = BPD * devices_all
    half_cap = CAP // 2
    key_owner = jax.random.fold_in(key, 11)
    key_split = jax.random.fold_in(key, 12)
    key_place = jax.random.fold_in(key, 13)
    owner_perm = jax.random.permutation(key_owner, devices_all)
    shifts = jax.random.randint(key_split, (devices_all // 2, BPD), -half_cap, half_cap + 1)
    shifts = shifts.at[0].set(half_cap)
    counts = jnp.zeros((devices_all, BPD), jnp.int32)
    counts = counts.at[owner_perm[0::2]].set(half_cap + shifts)
    counts = counts.at[owner_perm[1::2]].set(half_cap - shifts)
    counts = counts.reshape(bucket_total)
    listing = jnp.repeat(jnp.arange(bucket_total, dtype=jnp.int32), counts, total_repeat_length=FILES)
    per_device = listing.reshape(F_DEV, devices_all).T
    row_keys = jax.random.split(key_place, devices_all)
    orders = jax.vmap(lambda single: jax.random.permutation(single, F_DEV))(row_keys)
    per_device = jnp.take_along_axis(per_device, orders, axis=1)
    return per_device.reshape(FILES).astype(jnp.int32)


def draw_embeddings(key, part):
    key_base = jax.random.fold_in(key, 21)
    key_rows = jax.random.fold_in(key, 22)
    key_cols = jax.random.fold_in(key, 23)
    row_scale = jnp.exp(jax.random.uniform(key_rows, (FILES, 1), jnp.float32) * math.log(10.0))
    col_scale = jnp.exp(jax.random.uniform(key_cols, (1, D), jnp.float32) * math.log(10.0))
    base = jnp.clip(jax.random.normal(key_base, (FILES, D), jnp.float32), -6.0, 6.0)
    return (base * row_scale * col_scale / 10.0).astype(jnp.bfloat16)


def setup_inputs(seed: int = 0) -> dict:
    streams_of = jax.random.split(jax.random.key(seed), 3)
    return {
        "embeddings": draw_embeddings(jax.random.fold_in(streams_of[2], 71), 0),
        "bucket": draw_bucket(jax.random.fold_in(streams_of[2], 71), 0),
    }


sharpness = 32.0
epsilon = 1e-06

def inverse_norm(rows):
    return 1.0 / jnp.sqrt(lax.optimization_barrier(jnp.mean(jnp.square(rows.astype(jnp.float32)), axis=-1)) + epsilon)

def reference(embeddings, bucket):
    total_files = embeddings.shape[0]
    bucket_count = BPD * N_HX * N_HY
    file_index = jnp.arange(total_files, dtype=jnp.int32)
    file_order = jnp.argsort(bucket * total_files + file_index).astype(jnp.int32)
    sorted_bucket = bucket[file_order].astype(jnp.int32)
    per_bucket = jnp.zeros((bucket_count,), jnp.int32).at[bucket].add(1)
    starts = (jnp.cumsum(per_bucket) - per_bucket).astype(jnp.int32)
    rank_sorted = (file_index - starts[sorted_bucket]).astype(jnp.int32)
    block_rows = jnp.zeros((bucket_count, CAP, D), embeddings.dtype).at[sorted_bucket, rank_sorted].set(embeddings[file_order])
    block_file = jnp.full((bucket_count, CAP), -1, jnp.int32).at[sorted_bucket, rank_sorted].set(file_order)
    block_inv = jnp.zeros((bucket_count, CAP), jnp.float32).at[sorted_bucket, rank_sorted].set(inverse_norm(embeddings)[file_order])
    high_x = N_HX // 2 * N_HY * BPD
    high_y = N_HY // 2 * BPD

    def one_bucket(which):
        probes = jnp.stack([which, which ^ 1, which ^ high_x, which ^ high_y]).astype(jnp.int32)
        key_rows = block_rows[probes].reshape(4 * CAP, D)
        key_inv = block_inv[probes].reshape(4 * CAP)
        key_file = block_file[probes].reshape(4 * CAP)
        query_rows = block_rows[which]
        query_inv = block_inv[which]
        query_file = block_file[which]
        products = jnp.dot(query_rows, key_rows.T, preferred_element_type=jnp.float32)
        score = products * query_inv[:, None] * key_inv[None, :] * (sharpness / D)
        live = (key_file[None, :] >= 0) & (key_file[None, :] != query_file[:, None])
        kernel = jnp.where(live, jnp.exp(score), jnp.float32(0.0))
        kernel_low = kernel.astype(jnp.bfloat16)
        numerator = jnp.dot(kernel_low, key_rows, preferred_element_type=jnp.float32)
        denominator = 1.0 + lax.optimization_barrier(jnp.sum(kernel, axis=1))
        return (numerator / denominator[:, None]).astype(jnp.bfloat16)
    out_blocks = lax.map(one_bucket, jnp.arange(bucket_count, dtype=jnp.int32))
    rank_file = jnp.zeros((total_files,), jnp.int32).at[file_order].set(rank_sorted)
    return out_blocks[bucket, rank_file]
```

```python
import functools
import math

import jax
import jax.numpy as jnp
from jax import lax
from jax.experimental import pallas as pl
from jax.experimental.pallas import tpu as pltpu
from jax.sharding import PartitionSpec as P

MESH = pl.DeviceIdType.MESH

BPD = 2
CAP = 512
sharpness = 32.0
epsilon = 1e-06
EMPTY = 128.0
FAR = -1e30
TQ = 256


def kernel(
    count_hx,
    count_hy,
    rows_ref,
    bucket_ref,
    out_ref,
    send_buf,
    own_buf,
    hx_buf,
    hy_buf,
    back_buf,
    home_buf,
    keys,
    key_scale,
    key_bias,
    query_scale,
    numer,
    denom,
    send_sem,
    recv_sem,
    local_sem,
):
    devices = count_hx * count_hy
    files, width = rows_ref.shape
    slots = 8
    half_hx = count_hx // 2
    half_hy = count_hy // 2
    plane = 2 * count_hy
    planes = devices // plane
    my_hx = lax.axis_index("hx")
    my_hy = lax.axis_index("hy")
    me = my_hx * count_hy + my_hy
    other_hx = my_hx + 1 - 2 * (my_hx % 2)

    def owner_at(hx, hy):
        return ((hx % 2) * half_hx + hx // 2) * count_hy + hy

    my_owner = owner_at(my_hx, my_hy)

    def partner(step):
        core = step % 2
        dx = (step // 2) % 4
        dz = (step // 8) % 4
        dy = step // 32
        hx = ((my_hx // 2 + dy) % 4) * 2 + (my_hx + core) % 2
        hy = ((my_hy // 4 + dx) % 4) * 4 + (my_hy + dz) % 4
        return hx, hy

    barrier = pltpu.get_barrier_semaphore()

    def greet(step, carry):
        hx, hy = partner(step)
        pl.semaphore_signal(barrier, inc=1, device_id=(hx, hy), device_id_type=MESH)
        return carry

    lax.fori_loop(1, devices, greet, 0)

    bucket_row = bucket_ref[...]
    bucket_cols = jnp.broadcast_to(bucket_row.astype(jnp.float32), (128, files)).T
    rank = jnp.zeros((1, files), jnp.float32)
    lane = lax.broadcasted_iota(jnp.int32, (128, files), 1)
    sub = lax.broadcasted_iota(jnp.int32, (128, files), 0)
    bucket_f = bucket_row.astype(jnp.float32)
    for block in range(files // 128):
        col = bucket_cols[block * 128 : (block + 1) * 128, 0:1]
        same = (col == bucket_f) & (sub + block * 128 < lane)
        rank = rank + jnp.sum(jnp.where(same, 1.0, 0.0), axis=0, keepdims=True)
    target = bucket_f * 4.0 + rank
    slot_cols = jnp.broadcast_to(target, (128, files)).T

    rows = rows_ref[...]

    def pack(block, carry):
        place = lax.broadcasted_iota(jnp.int32, (256, files), 0) + block * 256
        match = (place.astype(jnp.float32) == target).astype(jnp.float32)
        used = jnp.sum(match, axis=1, keepdims=True)
        packed = jnp.dot(match.astype(jnp.bfloat16), rows, preferred_element_type=jnp.float32)
        packed = jnp.where(used > 0.5, packed, EMPTY)
        send_buf[pl.ds(block * 32, 32)] = packed.reshape(32, slots, width).astype(jnp.bfloat16)
        return carry

    lax.fori_loop(0, devices * slots // 256, pack, 0)

    pl.semaphore_wait(barrier, devices - 1)

    def send_own(step, carry):
        hx, hy = partner(step)
        pltpu.make_async_remote_copy(
            src_ref=send_buf.at[owner_at(hx, hy)],
            dst_ref=own_buf.at[me],
            send_sem=send_sem.at[0],
            recv_sem=recv_sem.at[0],
            device_id=(hx, hy),
            device_id_type=MESH,
        ).start()
        return carry

    def send_hy(step, carry):
        hx, hy = partner(step)
        pltpu.make_async_remote_copy(
            src_ref=send_buf.at[owner_at(hx, (hy + half_hy) % count_hy)],
            dst_ref=hy_buf.at[me],
            send_sem=send_sem.at[1],
            recv_sem=recv_sem.at[1],
            device_id=(hx, hy),
            device_id_type=MESH,
        ).start()
        return carry

    self_own = pltpu.make_async_copy(send_buf.at[my_owner], own_buf.at[me], local_sem.at[0])
    self_hy = pltpu.make_async_copy(
        send_buf.at[owner_at(my_hx, (my_hy + half_hy) % count_hy)], hy_buf.at[me], local_sem.at[1]
    )
    self_own.start()
    self_hy.start()
    lax.fori_loop(1, devices, send_own, 0)
    lax.fori_loop(1, devices, send_hy, 0)

    numer[...] = jnp.zeros_like(numer)
    denom[...] = jnp.zeros_like(denom)

    def wait_all(buf, sem):
        part = buf.at[pl.ds(0, devices - 1)]
        pltpu.make_async_copy(part, part, sem).wait()

    low = lax.broadcasted_iota(jnp.int32, (16, slots, width), 1) < 4
    fold = sharpness / width * math.log2(math.e)

    def mixed(one, two):
        first = jnp.where(low, one, pltpu.roll(two, 4, 1))
        second = jnp.where(low, pltpu.roll(one, 4, 1), two)
        return first, second

    def settle(source, base, with_query):
        def block_step(block, carry):
            taken = source[pl.ds(block * 32, 32)].astype(jnp.float32).reshape(16, 2, slots, width)
            pair = mixed(taken[:, 0], taken[:, 1])
            start = pl.multiple_of(block * 128, 128)
            for which in range(BPD):
                values = pair[which].reshape(128, width)
                square = jnp.sum(values * values, axis=1, keepdims=True)
                inverse = 1.0 / jnp.sqrt(square * (1.0 / width) + epsilon)
                used = values[:, 0:1] < 100.0
                wide = jnp.broadcast_to(jnp.where(used, inverse, -1.0), (128, 128))
                across = wide.T[0:1, :]
                keys[base + which, pl.ds(start, 128), :] = values.astype(jnp.bfloat16)
                key_scale[base + which, :, pl.ds(start, 128)] = across
                key_bias[base + which, :, pl.ds(start, 128)] = jnp.where(across > 0.0, 0.0, FAR)
                if with_query:
                    query_scale[base + which, pl.ds(start, 128), :] = jnp.broadcast_to(
                        inverse * fold, (128, 128)
                    )
            return carry

        lax.fori_loop(0, devices // 32, block_step, 0)

    def pair_tile(query, start, tile, key, skip_self):
        queries = keys[query, pl.ds(start, tile), :]
        against = keys[key]
        products = lax.dot_general(
            queries, against, (((1,), (1,)), ((), ())), preferred_element_type=jnp.float32
        )
        scale = query_scale[query, pl.ds(start, tile), :][:, 0:1]
        weight = jnp.exp2(products * scale * key_scale[key] + key_bias[key])
        if skip_self is not None:
            row = lax.broadcasted_iota(jnp.int32, (tile, CAP), 0) + start + skip_self
            col = lax.broadcasted_iota(jnp.int32, (tile, CAP), 1)
            weight = jnp.where(row == col, 0.0, weight)
        total = weight[:, 0:128]
        for part in range(1, CAP // 128):
            total = total + weight[:, part * 128 : (part + 1) * 128]
        summed = jnp.dot(weight.astype(jnp.bfloat16), against, preferred_element_type=jnp.float32)
        return summed, total

    def accumulate(query, start, tile, key, skip_self):
        summed, total = pair_tile(query, start, tile, key, skip_self)
        numer[query, pl.ds(start, tile), :] += summed
        denom[query, pl.ds(start, tile), :] += total

    wait_all(own_buf, recv_sem.at[0])
    self_own.wait()
    swap = pltpu.make_async_remote_copy(
        src_ref=own_buf,
        dst_ref=hx_buf,
        send_sem=send_sem.at[2],
        recv_sem=recv_sem.at[2],
        device_id=(other_hx, my_hy),
        device_id_type=MESH,
    )
    swap.start()
    settle(own_buf, 0, True)
    tiles = CAP // TQ

    def own_step(step, carry):
        query = step // (2 * tiles)
        key = (step // tiles) % 2
        start = pl.multiple_of((step % tiles) * TQ, TQ)
        apart = (query + key) % 2
        accumulate(query, start, TQ, key, apart * (2 * CAP))
        return carry

    lax.fori_loop(0, 4 * tiles, own_step, 0)

    swap.wait_recv()
    settle(hx_buf, 2, False)

    def hx_step(step, carry):
        query = step // tiles
        start = pl.multiple_of((step % tiles) * TQ, TQ)
        accumulate(query, start, TQ, 2 + query, None)
        return carry

    lax.fori_loop(0, 2 * tiles, hx_step, 0)

    wait_all(hy_buf, recv_sem.at[1])
    self_hy.wait()
    settle(hy_buf, 4, False)

    def last_step(step, carry):
        block = (my_hx // 2 + step) % planes
        start = pl.multiple_of(block * 128, 128)
        pieces = []
        for query in range(BPD):
            summed, total = pair_tile(query, start, 128, 4 + query, None)
            whole = numer[query, pl.ds(start, 128), :] + summed
            under = denom[query, pl.ds(start, 128), :] + total
            under = 1.0 + jnp.sum(under, axis=1, keepdims=True)
            pieces.append((whole * (1.0 / under)).reshape(16, slots, width))
        first, second = mixed(pieces[0], pieces[1])
        both = jnp.stack([first, second], axis=1).reshape(32, slots, width)
        back_buf[pl.ds(block * plane, plane)] = both.astype(jnp.bfloat16)

        def give(index, inner):
            core = index % 2
            hx = block * 2 + (my_hx + core) % 2
            dx = (index // 2) % 4
            dz = index // 8
            hy = ((my_hy // 4 + dx) % 4) * 4 + (my_hy + dz) % 4
            to = hx * count_hy + hy

            @pl.when(to != me)
            def _():
                pltpu.make_async_remote_copy(
                    src_ref=back_buf.at[to],
                    dst_ref=home_buf.at[my_owner],
                    send_sem=send_sem.at[3],
                    recv_sem=recv_sem.at[3],
                    device_id=(hx, hy),
                    device_id_type=MESH,
                ).start()

            return inner

        lax.fori_loop(0, plane, give, 0)
        return carry

    lax.fori_loop(0, planes, last_step, 0)
    self_back = pltpu.make_async_copy(back_buf.at[me], home_buf.at[my_owner], local_sem.at[2])
    self_back.start()
    self_back.wait()
    wait_all(home_buf, recv_sem.at[3])

    result = jnp.zeros((files, width), jnp.float32)
    slot_wide = jnp.concatenate([slot_cols, slot_cols], axis=1)
    place = lax.broadcasted_iota(jnp.int32, (files, 256), 1).astype(jnp.float32)
    for block in range(devices * slots // 256):
        match = (slot_wide == place + float(block * 256)).astype(jnp.float32)
        got = home_buf[pl.ds(block * 32, 32)].astype(jnp.float32).reshape(256, width)
        result = result + jnp.dot(
            match.astype(jnp.bfloat16), got.astype(jnp.bfloat16), preferred_element_type=jnp.float32
        )
    out_ref[...] = result.astype(jnp.bfloat16)

    swap.wait_send()
    wait_all(send_buf, send_sem.at[0])
    wait_all(send_buf, send_sem.at[1])
    wait_all(back_buf, send_sem.at[3])


def solution(mesh):
    count_hx = mesh.shape["hx"]
    count_hy = mesh.shape["hy"]
    devices = count_hx * count_hy

    def body(embeddings, bucket):
        files, width = embeddings.shape
        chunk = (devices, 8, width)
        return pl.pallas_call(
            functools.partial(kernel, count_hx, count_hy),
            out_shape=jax.ShapeDtypeStruct((files, width), jnp.bfloat16),
            in_specs=[pl.BlockSpec(memory_space=pltpu.VMEM)] * 2,
            out_specs=pl.BlockSpec(memory_space=pltpu.VMEM),
            scratch_shapes=[
                pltpu.VMEM(chunk, jnp.bfloat16),
                pltpu.VMEM(chunk, jnp.bfloat16),
                pltpu.VMEM(chunk, jnp.bfloat16),
                pltpu.VMEM(chunk, jnp.bfloat16),
                pltpu.VMEM(chunk, jnp.bfloat16),
                pltpu.VMEM(chunk, jnp.bfloat16),
                pltpu.VMEM((6, CAP, width), jnp.bfloat16),
                pltpu.VMEM((6, 1, CAP), jnp.float32),
                pltpu.VMEM((6, 1, CAP), jnp.float32),
                pltpu.VMEM((2, CAP, 128), jnp.float32),
                pltpu.VMEM((2, CAP, width), jnp.float32),
                pltpu.VMEM((2, CAP, 128), jnp.float32),
                pltpu.SemaphoreType.DMA((4,)),
                pltpu.SemaphoreType.DMA((4,)),
                pltpu.SemaphoreType.DMA((3,)),
            ],
            compiler_params=pltpu.CompilerParams(
                collective_id=0, has_side_effects=True, vmem_limit_bytes=60 * 1024 * 1024
            ),
        )(embeddings, bucket.reshape(1, files))

    return jax.shard_map(
        body,
        mesh=mesh,
        in_specs=(P(("hx", "hy"), None), P(("hx", "hy"))),
        out_specs=P(("hx", "hy"), None),
        check_vma=False,
    )
```

```python
import functools
import math

import jax
import jax.numpy as jnp
from jax import lax
from jax.experimental import pallas as pl
from jax.experimental.pallas import tpu as pltpu
from jax.sharding import PartitionSpec as P

MESH = pl.DeviceIdType.MESH

BPD = 2
CAP = 512
sharpness = 32.0
epsilon = 1e-06
EMPTY = 128.0
FAR = -1e30
TQ = 256


def kernel(
    count_hx,
    count_hy,
    rows_ref,
    bucket_ref,
    out_ref,
    send_buf,
    own_buf,
    hx_buf,
    hy_buf,
    back_buf,
    home_buf,
    keys,
    key_scale,
    key_bias,
    query_scale,
    numer,
    denom,
    send_sem,
    recv_sem,
    local_sem,
):
    devices = count_hx * count_hy
    files, width = rows_ref.shape
    slots = 8
    half_hx = count_hx // 2
    half_hy = count_hy // 2
    plane = 2 * count_hy
    planes = devices // plane
    my_hx = lax.axis_index("hx")
    my_hy = lax.axis_index("hy")
    me = my_hx * count_hy + my_hy
    other_hx = my_hx + 1 - 2 * (my_hx % 2)

    def owner_at(hx, hy):
        return ((hx % 2) * half_hx + hx // 2) * count_hy + hy

    my_owner = owner_at(my_hx, my_hy)

    def partner(step):
        core = step // 64
        dx = step % 4
        dy = (step // 4 + step) % 4
        dz = (step // 16 + step // 4 + step) % 4
        hx = ((my_hx // 2 + dy) % 4) * 2 + (my_hx + core) % 2
        hy = ((my_hy // 4 + dx) % 4) * 4 + (my_hy + dz) % 4
        return hx, hy

    barrier = pltpu.get_barrier_semaphore()

    hxs = [(my_hx // 2 + dy) % 4 * 2 + (my_hx + core) % 2 for dy in range(4) for core in range(2)]
    hys = [(my_hy // 4 + dx) % 4 * 4 + (my_hy + dz) % 4 for dx in range(4) for dz in range(4)]
    for row in reversed(range(8)):
        for column in reversed(range(16)):
            if row or column:
                pl.semaphore_signal(
                    barrier, inc=1, device_id=(hxs[row], hys[column]), device_id_type=MESH
                )

    bucket_row = bucket_ref[...]
    bucket_cols = jnp.broadcast_to(bucket_row.astype(jnp.float32), (128, files)).T
    rank = jnp.zeros((1, files), jnp.float32)
    lane = lax.broadcasted_iota(jnp.int32, (128, files), 1)
    sub = lax.broadcasted_iota(jnp.int32, (128, files), 0)
    bucket_f = bucket_row.astype(jnp.float32)
    for block in range(files // 128):
        col = bucket_cols[block * 128 : (block + 1) * 128, 0:1]
        same = (col == bucket_f) & (sub + block * 128 < lane)
        rank = rank + jnp.sum(jnp.where(same, 1.0, 0.0), axis=0, keepdims=True)
    target = bucket_f * 4.0 + rank
    slot_cols = jnp.broadcast_to(target, (128, files)).T

    rows = rows_ref[...]

    def pack(block, carry):
        place = lax.broadcasted_iota(jnp.int32, (256, files), 0) + block * 256
        match = (place.astype(jnp.float32) == target).astype(jnp.float32)
        used = jnp.sum(match, axis=1, keepdims=True)
        packed = jnp.dot(match.astype(jnp.bfloat16), rows, preferred_element_type=jnp.float32)
        packed = jnp.where(used > 0.5, packed, EMPTY)
        send_buf[pl.ds(block * 32, 32)] = packed.reshape(32, slots, width).astype(jnp.bfloat16)
        return carry

    lax.fori_loop(0, devices * slots // 256, pack, 0)

    pl.semaphore_wait(barrier, devices - 1)

    def send_own(step, carry):
        hx, hy = partner(step)
        pltpu.make_async_remote_copy(
            src_ref=send_buf.at[owner_at(hx, hy)],
            dst_ref=own_buf.at[me],
            send_sem=send_sem.at[0],
            recv_sem=recv_sem.at[0],
            device_id=(hx, hy),
            device_id_type=MESH,
        ).start()
        return carry

    def send_hy(step, carry):
        hx, hy = partner(step)
        pltpu.make_async_remote_copy(
            src_ref=send_buf.at[owner_at(hx, (hy + half_hy) % count_hy)],
            dst_ref=hy_buf.at[me],
            send_sem=send_sem.at[1],
            recv_sem=recv_sem.at[1],
            device_id=(hx, hy),
            device_id_type=MESH,
        ).start()
        return carry

    self_own = pltpu.make_async_copy(send_buf.at[my_owner], own_buf.at[me], local_sem.at[0])
    self_hy = pltpu.make_async_copy(
        send_buf.at[owner_at(my_hx, (my_hy + half_hy) % count_hy)], hy_buf.at[me], local_sem.at[1]
    )
    self_own.start()
    self_hy.start()
    lax.fori_loop(1, devices, send_own, 0)
    lax.fori_loop(1, devices, send_hy, 0)

    numer[...] = jnp.zeros_like(numer)
    denom[...] = jnp.zeros_like(denom)

    def wait_all(buf, sem):
        part = buf.at[pl.ds(0, devices - 1)]
        pltpu.make_async_copy(part, part, sem).wait()

    low = lax.broadcasted_iota(jnp.int32, (16, slots, width), 1) < 4
    fold = sharpness / width * math.log2(math.e)

    def mixed(one, two):
        first = jnp.where(low, one, pltpu.roll(two, 4, 1))
        second = jnp.where(low, pltpu.roll(one, 4, 1), two)
        return first, second

    def settle(source, base, with_query):
        def block_step(block, carry):
            taken = source[pl.ds(block * 32, 32)].astype(jnp.float32).reshape(16, 2, slots, width)
            pair = mixed(taken[:, 0], taken[:, 1])
            start = pl.multiple_of(block * 128, 128)
            for which in range(BPD):
                values = pair[which].reshape(128, width)
                square = jnp.sum(values * values, axis=1, keepdims=True)
                inverse = 1.0 / jnp.sqrt(square * (1.0 / width) + epsilon)
                used = values[:, 0:1] < 100.0
                wide = jnp.broadcast_to(jnp.where(used, inverse, -1.0), (128, 128))
                across = wide.T[0:1, :]
                keys[base + which, pl.ds(start, 128), :] = values.astype(jnp.bfloat16)
                key_scale[base + which, :, pl.ds(start, 128)] = across
                key_bias[base + which, :, pl.ds(start, 128)] = jnp.where(across > 0.0, 0.0, FAR)
                if with_query:
                    query_scale[base + which, pl.ds(start, 128), :] = jnp.broadcast_to(
                        inverse * fold, (128, 128)
                    )
            return carry

        lax.fori_loop(0, devices // 32, block_step, 0)

    def pair_tile(query, start, tile, key, skip_self):
        queries = keys[query, pl.ds(start, tile), :]
        against = keys[key]
        products = lax.dot_general(
            queries, against, (((1,), (1,)), ((), ())), preferred_element_type=jnp.float32
        )
        scale = query_scale[query, pl.ds(start, tile), :][:, 0:1]
        weight = jnp.exp2(products * scale * key_scale[key] + key_bias[key])
        if skip_self is not None:
            row = lax.broadcasted_iota(jnp.int32, (tile, CAP), 0) + start + skip_self
            col = lax.broadcasted_iota(jnp.int32, (tile, CAP), 1)
            weight = jnp.where(row == col, 0.0, weight)
        total = weight[:, 0:128]
        for part in range(1, CAP // 128):
            total = total + weight[:, part * 128 : (part + 1) * 128]
        summed = jnp.dot(weight.astype(jnp.bfloat16), against, preferred_element_type=jnp.float32)
        return summed, total

    def accumulate(query, start, tile, key, skip_self):
        summed, total = pair_tile(query, start, tile, key, skip_self)
        numer[query, pl.ds(start, tile), :] += summed
        denom[query, pl.ds(start, tile), :] += total

    wait_all(own_buf, recv_sem.at[0])
    self_own.wait()
    swap = pltpu.make_async_remote_copy(
        src_ref=own_buf,
        dst_ref=hx_buf,
        send_sem=send_sem.at[2],
        recv_sem=recv_sem.at[2],
        device_id=(other_hx, my_hy),
        device_id_type=MESH,
    )
    swap.start()
    settle(own_buf, 0, True)
    tiles = CAP // TQ

    def own_step(step, carry):
        query = step // (2 * tiles)
        key = (step // tiles) % 2
        start = pl.multiple_of((step % tiles) * TQ, TQ)
        apart = (query + key) % 2
        accumulate(query, start, TQ, key, apart * (2 * CAP))
        return carry

    lax.fori_loop(0, 4 * tiles, own_step, 0)

    swap.wait_recv()
    settle(hx_buf, 2, False)

    def hx_step(step, carry):
        query = step // tiles
        start = pl.multiple_of((step % tiles) * TQ, TQ)
        accumulate(query, start, TQ, 2 + query, None)
        return carry

    lax.fori_loop(0, 2 * tiles, hx_step, 0)

    wait_all(hy_buf, recv_sem.at[1])
    self_hy.wait()
    settle(hy_buf, 4, False)

    def last_step(step, carry):
        block = (my_hx // 2 + 2 + 3 * step) % planes
        start = pl.multiple_of(block * 128, 128)
        pieces = []
        for query in range(BPD):
            summed, total = pair_tile(query, start, 128, 4 + query, None)
            whole = numer[query, pl.ds(start, 128), :] + summed
            under = denom[query, pl.ds(start, 128), :] + total
            under = 1.0 + jnp.sum(under, axis=1, keepdims=True)
            pieces.append((whole * (1.0 / under)).reshape(16, slots, width))
        first, second = mixed(pieces[0], pieces[1])
        both = jnp.stack([first, second], axis=1).reshape(32, slots, width)
        back_buf[pl.ds(block * plane, plane)] = both.astype(jnp.bfloat16)

        def give(index, inner):
            core = index // 16
            hx = block * 2 + (my_hx + core) % 2
            dx = (index + 2) % 4
            dz = (index // 4 + index) % 4
            hy = ((my_hy // 4 + dx) % 4) * 4 + (my_hy + dz) % 4
            to = hx * count_hy + hy

            @pl.when(to != me)
            def _():
                pltpu.make_async_remote_copy(
                    src_ref=back_buf.at[to],
                    dst_ref=home_buf.at[my_owner],
                    send_sem=send_sem.at[3],
                    recv_sem=recv_sem.at[3],
                    device_id=(hx, hy),
                    device_id_type=MESH,
                ).start()

            return inner

        lax.fori_loop(0, plane, give, 0)
        return carry

    lax.fori_loop(0, planes, last_step, 0)
    self_back = pltpu.make_async_copy(back_buf.at[me], home_buf.at[my_owner], local_sem.at[2])
    self_back.start()
    self_back.wait()
    wait_all(home_buf, recv_sem.at[3])

    result = jnp.zeros((files, width), jnp.float32)
    slot_wide = jnp.concatenate([slot_cols, slot_cols], axis=1)
    place = lax.broadcasted_iota(jnp.int32, (files, 256), 1).astype(jnp.float32)
    for block in range(devices * slots // 256):
        match = (slot_wide == place + float(block * 256)).astype(jnp.float32)
        got = home_buf[pl.ds(block * 32, 32)].astype(jnp.float32).reshape(256, width)
        result = result + jnp.dot(
            match.astype(jnp.bfloat16), got.astype(jnp.bfloat16), preferred_element_type=jnp.float32
        )
    out_ref[...] = result.astype(jnp.bfloat16)

    swap.wait_send()
    wait_all(send_buf, send_sem.at[0])
    wait_all(send_buf, send_sem.at[1])
    wait_all(back_buf, send_sem.at[3])


def solution(mesh):
    count_hx = mesh.shape["hx"]
    count_hy = mesh.shape["hy"]
    devices = count_hx * count_hy

    def body(embeddings, bucket):
        files, width = embeddings.shape
        chunk = (devices, 8, width)
        return pl.pallas_call(
            functools.partial(kernel, count_hx, count_hy),
            out_shape=jax.ShapeDtypeStruct((files, width), jnp.bfloat16),
            in_specs=[pl.BlockSpec(memory_space=pltpu.VMEM)] * 2,
            out_specs=pl.BlockSpec(memory_space=pltpu.VMEM),
            scratch_shapes=[
                pltpu.VMEM(chunk, jnp.bfloat16),
                pltpu.VMEM(chunk, jnp.bfloat16),
                pltpu.VMEM(chunk, jnp.bfloat16),
                pltpu.VMEM(chunk, jnp.bfloat16),
                pltpu.VMEM(chunk, jnp.bfloat16),
                pltpu.VMEM(chunk, jnp.bfloat16),
                pltpu.VMEM((6, CAP, width), jnp.bfloat16),
                pltpu.VMEM((6, 1, CAP), jnp.float32),
                pltpu.VMEM((6, 1, CAP), jnp.float32),
                pltpu.VMEM((2, CAP, 128), jnp.float32),
                pltpu.VMEM((2, CAP, width), jnp.float32),
                pltpu.VMEM((2, CAP, 128), jnp.float32),
                pltpu.SemaphoreType.DMA((4,)),
                pltpu.SemaphoreType.DMA((4,)),
                pltpu.SemaphoreType.DMA((3,)),
            ],
            compiler_params=pltpu.CompilerParams(
                collective_id=0, has_side_effects=True, vmem_limit_bytes=60 * 1024 * 1024
            ),
        )(embeddings, bucket.reshape(1, files))

    return jax.shard_map(
        body,
        mesh=mesh,
        in_specs=(P(("hx", "hy"), None), P(("hx", "hy"))),
        out_specs=P(("hx", "hy"), None),
        check_vma=False,
    )
```

```python
import functools
import math

import jax
import jax.numpy as jnp
from jax import lax
from jax.experimental import pallas as pl
from jax.experimental.pallas import tpu as pltpu
from jax.sharding import PartitionSpec as P

MESH = pl.DeviceIdType.MESH

CAP = 512
BUCKETS = 256
SLOTS = 4
sharpness = 32.0
epsilon = 1e-06
EMPTY = 128.0
FAR = -1e30
TQ = 256

OFFSET = {name: 128 * (name // 100) + 16 * (name // 10 % 10) + name % 10 for name in (0, 1, 10, 11, 100, 101, 110)}
DIRECT = ((0, 1, 101), (10, 100, 11, 110))


def rem(value, by):
    return lax.rem(value, jnp.int32(by))


def div(value, by):
    return lax.div(value, jnp.int32(by))


def kernel(
    rows_ref,
    bucket_ref,
    out_ref,
    send_buf,
    raw,
    back_buf,
    home_buf,
    keys,
    key_scale,
    key_bias,
    query_scale,
    numer,
    denom,
    send_sem,
    recv_sem,
    local_sem,
):
    files, width = rows_ref.shape
    devices = raw.shape[1]
    half = width // 2
    my_hx = lax.axis_index("hx")
    my_hy = lax.axis_index("hy")
    my_core = rem(my_hx, 2)
    my_y = div(my_hx, 2)
    my_x = div(my_hy, 4)
    my_z = rem(my_hy, 4)
    me = my_hx * 16 + my_hy

    def bucket_at(y, hy, name):
        offset = OFFSET[name]
        return 32 * y + 2 * rem(hy, 8) + offset + div(hy, 8) * (145 - 2 * offset)

    def chip(step):
        first, second, third = rem(step, 4), div(step, 4), div(step, 16)
        x = rem(my_x + first, 4)
        y = rem(my_y + second + first, 4)
        z = rem(my_z + third + second + first, 4)
        return y, x * 4 + z

    barrier = pltpu.get_barrier_semaphore()
    hxs = [rem(my_y + dy, 4) * 2 + rem(my_core + core, 2) for dy in range(4) for core in range(2)]
    hys = [rem(my_x + dx, 4) * 4 + rem(my_z + dz, 4) for dx in range(4) for dz in range(4)]
    for row in reversed(range(8)):
        for column in reversed(range(16)):
            if row or column:
                pl.semaphore_signal(
                    barrier, inc=1, device_id=(hxs[row], hys[column]), device_id_type=MESH
                )

    bucket_f = bucket_ref[...].astype(jnp.float32)
    bucket_cols = jnp.broadcast_to(bucket_f, (128, files)).T
    rank = jnp.zeros((1, files), jnp.float32)
    lane = lax.broadcasted_iota(jnp.int32, (128, files), 1)
    sub = lax.broadcasted_iota(jnp.int32, (128, files), 0)
    for block in range(files // 128):
        col = bucket_cols[block * 128 : (block + 1) * 128, 0:1]
        same = (col == bucket_f) & (sub + block * 128 < lane)
        rank = rank + jnp.sum(jnp.where(same, 1.0, 0.0), axis=0, keepdims=True)
    target = bucket_f * float(SLOTS) + rank
    slot_cols = jnp.broadcast_to(target, (128, files)).T

    def mixed(one, two):
        low = lax.broadcasted_iota(jnp.int32, one.shape, 1) < SLOTS
        first = jnp.where(low, one, pltpu.roll(two, SLOTS, 1))
        second = jnp.where(low, pltpu.roll(one, SLOTS, 1), two)
        return first, second

    def fold_rows(values):
        count = values.shape[0] // 8
        one, two = mixed(
            values[:, :half].reshape(count, 8, half), values[:, half:].reshape(count, 8, half)
        )
        return jnp.stack([one, two], axis=1).reshape(count * 2, 8, half).astype(jnp.bfloat16)

    def unfold_rows(packed):
        count = packed.shape[0] // 2
        halves = packed.astype(jnp.float32).reshape(count, 2, 8, half)
        first, second = mixed(halves[:, 0], halves[:, 1])
        return first.reshape(count * 8, half), second.reshape(count * 8, half)

    rows = rows_ref[...]

    def pack(block, carry):
        place = lax.broadcasted_iota(jnp.int32, (256, files), 0) + block * 256
        match = (place.astype(jnp.float32) == target).astype(jnp.float32)
        used = jnp.sum(match, axis=1, keepdims=True)
        packed = jnp.dot(match.astype(jnp.bfloat16), rows, preferred_element_type=jnp.float32)
        send_buf[pl.ds(block * 64, 64)] = fold_rows(jnp.where(used > 0.5, packed, EMPTY))
        return carry

    lax.fori_loop(0, BUCKETS * SLOTS // 256, pack, 0)

    pl.semaphore_wait(barrier, devices - 1)

    def send(y, hy, core, slot):
        pltpu.make_async_remote_copy(
            src_ref=send_buf.at[bucket_at(y, hy, DIRECT[core][slot])],
            dst_ref=raw.at[slot, me],
            send_sem=send_sem.at[slot],
            recv_sem=recv_sem.at[slot],
            device_id=(y * 2 + core, hy),
            device_id_type=MESH,
        ).start()

    def keep(core, slot):
        return pltpu.make_async_copy(
            send_buf.at[bucket_at(my_y, my_hy, DIRECT[core][slot])],
            raw.at[slot, me],
            local_sem.at[slot],
        )

    for core in range(2):

        @pl.when(my_core == core)
        def _():
            for slot in range(len(DIRECT[core])):
                keep(core, slot).start()
            for slot in range(len(DIRECT[1 - core])):
                send(my_y, my_hy, 1 - core, slot)

    def send_first(step, carry):
        y, hy = chip(step)
        for core in range(2):
            for slot in range(2):
                send(y, hy, core, slot)
        return carry

    def send_second(step, carry):
        y, hy = chip(step)
        for core in range(2):
            send(y, hy, core, 2)
        return carry

    def send_third(step, carry):
        y, hy = chip(step)
        send(y, hy, 1, 3)
        return carry

    chips = devices // 2
    lax.fori_loop(1, chips, send_first, 0)
    lax.fori_loop(1, chips, send_second, 0)
    lax.fori_loop(1, chips, send_third, 0)

    def wait_count(buf, count, sem):
        part = buf.at[pl.ds(0, count)]
        pltpu.make_async_copy(part, part, sem).wait()

    def wait_slot(slot):
        wait_count(raw.at[slot], devices - 1, recv_sem.at[slot])

    def share(slot, there, sem):
        return pltpu.make_async_remote_copy(
            src_ref=raw.at[slot],
            dst_ref=raw.at[there],
            send_sem=send_sem.at[sem],
            recv_sem=recv_sem.at[there],
            device_id=(my_y * 2 + 1 - my_core, my_hy),
            device_id_type=MESH,
        )

    def wait_shared(slot):
        wait_count(raw.at[slot], devices, recv_sem.at[slot])

    scale_fold = sharpness / width * math.log2(math.e)

    def settle(slot, with_query):
        def block_step(block, carry):
            first, second = unfold_rows(raw[slot, pl.ds(block * 32, 32)])
            start = pl.multiple_of(block * 128, 128)
            square = jnp.sum(first * first + second * second, axis=1, keepdims=True)
            inverse = 1.0 / jnp.sqrt(square * (1.0 / width) + epsilon)
            used = first[:, 0:1] < 100.0
            wide = jnp.broadcast_to(jnp.where(used, inverse, -1.0), (128, 128))
            across = wide.T[0:1, :]
            keys[slot, pl.ds(start, 128), 0:half] = first.astype(jnp.bfloat16)
            keys[slot, pl.ds(start, 128), half:width] = second.astype(jnp.bfloat16)
            key_scale[slot, :, pl.ds(start, 128)] = across
            key_bias[slot, :, pl.ds(start, 128)] = jnp.where(across > 0.0, 0.0, FAR)
            if with_query:
                query_scale[slot, pl.ds(start, 128), :] = jnp.broadcast_to(
                    inverse * scale_fold, (128, 128)
                )
            return carry

        lax.fori_loop(0, devices // 32, block_step, 0)

    def pair_tile(query, start, tile, key, skip_self):
        queries = keys[query, pl.ds(start, tile), :]
        against = keys[key]
        products = lax.dot_general(
            queries, against, (((1,), (1,)), ((), ())), preferred_element_type=jnp.float32
        )
        scale = query_scale[query, pl.ds(start, tile), :][:, 0:1]
        weight = jnp.exp2(products * scale * key_scale[key] + key_bias[key])
        if skip_self:
            row = lax.broadcasted_iota(jnp.int32, (tile, CAP), 0) + start
            col = lax.broadcasted_iota(jnp.int32, (tile, CAP), 1)
            weight = jnp.where(row == col, 0.0, weight)
        total = weight[:, 0:128]
        for part in range(1, CAP // 128):
            total = total + weight[:, part * 128 : (part + 1) * 128]
        summed = jnp.dot(weight.astype(jnp.bfloat16), against, preferred_element_type=jnp.float32)
        return summed, total

    tiles = CAP // TQ

    def own_pairs():
        def step_of(step, carry):
            query = div(step, tiles)
            start = pl.multiple_of(rem(step, tiles) * TQ, TQ)
            summed, total = pair_tile(query, start, TQ, query, True)
            numer[query, pl.ds(start, TQ), :] = summed
            denom[query, pl.ds(start, TQ), :] = total
            return carry

        lax.fori_loop(0, 2 * tiles, step_of, 0)

    def pairs(count, which):
        def step_of(step, carry):
            query, key = which(div(step, tiles))
            start = pl.multiple_of(rem(step, tiles) * TQ, TQ)
            summed, total = pair_tile(query, start, TQ, key, False)
            numer[query, pl.ds(start, TQ), :] += summed
            denom[query, pl.ds(start, TQ), :] += total
            return carry

        lax.fori_loop(0, count * tiles, step_of, 0)

    def finish(query, key, name):
        mine = bucket_at(my_y, my_hy, name)

        def block_step(step, carry):
            y = rem(my_y + 2 + 3 * step, 4)
            start = pl.multiple_of(y * 128, 128)
            summed, total = pair_tile(query, start, 128, key, False)
            whole = numer[query, pl.ds(start, 128), :] + summed
            under = denom[query, pl.ds(start, 128), :] + total
            under = 1.0 + jnp.sum(under, axis=1, keepdims=True)
            back_buf[query, pl.ds(y * 32, 32)] = fold_rows(whole * (1.0 / under))

            def give(index, inner):
                x = rem(my_x + 2 + index, 4)
                z = rem(my_z + div(index, 4) + index, 4)
                hy = x * 4 + z
                for core in range(2):
                    to = (y * 2 + core) * 16 + hy

                    @pl.when(to != me)
                    def _():
                        pltpu.make_async_remote_copy(
                            src_ref=back_buf.at[query, to],
                            dst_ref=home_buf.at[mine],
                            send_sem=send_sem.at[7 + query],
                            recv_sem=recv_sem.at[6],
                            device_id=(y * 2 + core, hy),
                            device_id_type=MESH,
                        ).start()

                return inner

            lax.fori_loop(0, 16, give, 0)
            return carry

        lax.fori_loop(0, 4, block_step, 0)
        return pltpu.make_async_copy(back_buf.at[query, me], home_buf.at[mine], local_sem.at[4 + query])

    for slot in range(2):
        wait_slot(slot)
        keep(0, slot).wait()

    for core in range(2):

        @pl.when(my_core == core)
        def _():
            if core == 0:
                first_share = [share(0, 4, 4)]
            else:
                first_share = [share(0, 3, 4), share(1, 4, 5)]
            for copy in first_share:
                copy.start()
            settle(0, True)
            settle(1, True)
            own_pairs()
            if core == 0:
                pairs(2, lambda index: (index, 1 - index))
                wait_shared(3)
                settle(3, False)
                pairs(1, lambda index: (0, 3))
                wait_shared(4)
                settle(4, False)
                kept = [finish(0, 4, DIRECT[0][0])]
                kept[0].start()
                wait_slot(2)
                keep(0, 2).wait()
                second_share = share(2, 5, 6)
                second_share.start()
                settle(2, False)
                pairs(1, lambda index: (1, 2))
                wait_shared(5)
                settle(5, False)
                kept.append(finish(1, 5, DIRECT[0][1]))
                kept[1].start()
            else:
                wait_shared(4)
                settle(4, False)
                pairs(2, lambda index: (index, 4))
                wait_slot(2)
                keep(1, 2).wait()
                second_share = share(2, 5, 6)
                second_share.start()
                settle(2, False)
                pairs(1, lambda index: (0, 2))
                wait_shared(5)
                settle(5, False)
                pairs(1, lambda index: (1, 5))
                wait_slot(3)
                keep(1, 3).wait()
                settle(3, False)
                kept = [finish(0, 3, DIRECT[1][0])]
                kept[0].start()
                kept.append(finish(1, 3, DIRECT[1][1]))
                kept[1].start()
            for copy in kept:
                copy.wait()
            for copy in first_share:
                copy.wait_send()
            second_share.wait_send()

    got = home_buf.at[pl.ds(0, BUCKETS - 2)]
    pltpu.make_async_copy(got, got, recv_sem.at[6]).wait()

    slot_wide = jnp.concatenate([slot_cols, slot_cols], axis=1)
    place = lax.broadcasted_iota(jnp.int32, (files, 256), 1).astype(jnp.float32)
    results = [jnp.zeros((files, half), jnp.float32) for _ in range(2)]
    for block in range(BUCKETS * SLOTS // 256):
        match = (slot_wide == place + float(block * 256)).astype(jnp.float32).astype(jnp.bfloat16)
        parts = unfold_rows(home_buf[pl.ds(block * 64, 64)])
        results = [
            result + jnp.dot(match, part.astype(jnp.bfloat16), preferred_element_type=jnp.float32)
            for result, part in zip(results, parts)
        ]
    out_ref[:, 0:half] = results[0].astype(jnp.bfloat16)
    out_ref[:, half:width] = results[1].astype(jnp.bfloat16)

    for slot in range(3):
        wait_count(raw.at[slot], devices - 1, send_sem.at[slot])
    for core in range(2):

        @pl.when(my_core == core)
        def _():
            wait_count(raw.at[3], chips - core, send_sem.at[3])

    for query in range(2):
        wait_count(raw.at[query], devices - 1, send_sem.at[7 + query])


def solution(mesh):
    devices = mesh.shape["hx"] * mesh.shape["hy"]

    def body(embeddings, bucket):
        files, width = embeddings.shape
        half = width // 2
        return pl.pallas_call(
            kernel,
            out_shape=jax.ShapeDtypeStruct((files, width), jnp.bfloat16),
            in_specs=[pl.BlockSpec(memory_space=pltpu.VMEM)] * 2,
            out_specs=pl.BlockSpec(memory_space=pltpu.VMEM),
            scratch_shapes=[
                pltpu.VMEM((BUCKETS, 8, half), jnp.bfloat16),
                pltpu.VMEM((6, devices, 8, half), jnp.bfloat16),
                pltpu.VMEM((2, devices, 8, half), jnp.bfloat16),
                pltpu.VMEM((BUCKETS, 8, half), jnp.bfloat16),
                pltpu.VMEM((6, CAP, width), jnp.bfloat16),
                pltpu.VMEM((6, 1, CAP), jnp.float32),
                pltpu.VMEM((6, 1, CAP), jnp.float32),
                pltpu.VMEM((2, CAP, 128), jnp.float32),
                pltpu.VMEM((2, CAP, width), jnp.float32),
                pltpu.VMEM((2, CAP, 128), jnp.float32),
                pltpu.SemaphoreType.DMA((9,)),
                pltpu.SemaphoreType.DMA((7,)),
                pltpu.SemaphoreType.DMA((6,)),
            ],
            compiler_params=pltpu.CompilerParams(
                collective_id=0, has_side_effects=True, vmem_limit_bytes=60 * 1024 * 1024
            ),
        )(embeddings, bucket.reshape(1, files))

    return jax.shard_map(
        body,
        mesh=mesh,
        in_specs=(P(("hx", "hy"), None), P(("hx", "hy"))),
        out_specs=P(("hx", "hy"), None),
        check_vma=False,
    )
```

```python
import functools
import math

import jax
import jax.numpy as jnp
from jax import lax
from jax.experimental import pallas as pl
from jax.experimental.pallas import tpu as pltpu
from jax.sharding import PartitionSpec as P

MESH = pl.DeviceIdType.MESH

CAP = 512
BUCKETS = 256
SLOTS = 4
sharpness = 32.0
epsilon = 1e-06
EMPTY = 128.0
FAR = -1e30
SPAN = 64

OFFSET = {name: 128 * (name // 100) + 16 * (name // 10 % 10) + name % 10 for name in (0, 1, 10, 11, 100, 101, 110)}
DIRECT = ((0, 1, 101), (10, 100, 11, 110))


def rem(value, by):
    return lax.rem(value, jnp.int32(by))


def div(value, by):
    return lax.div(value, jnp.int32(by))


def kernel(
    rows_ref,
    bucket_ref,
    out_ref,
    send_buf,
    raw,
    back_buf,
    home_buf,
    keys,
    key_scale,
    key_bias,
    query_scale,
    numer,
    denom,
    send_sem,
    recv_sem,
    local_sem,
):
    files, width = rows_ref.shape
    devices = raw.shape[1]
    half = width // 2
    my_hx = lax.axis_index("hx")
    my_hy = lax.axis_index("hy")
    my_core = rem(my_hx, 2)
    my_y = div(my_hx, 2)
    my_x = div(my_hy, 4)
    my_z = rem(my_hy, 4)
    me = my_hx * 16 + my_hy

    def bucket_at(y, hy, name):
        offset = OFFSET[name]
        return 32 * y + 2 * rem(hy, 8) + offset + div(hy, 8) * (145 - 2 * offset)

    barrier = pltpu.get_barrier_semaphore()
    hxs = [rem(my_y + dy, 4) * 2 + rem(my_core + core, 2) for dy in range(4) for core in range(2)]
    hys = [rem(my_x + dx, 4) * 4 + rem(my_z + dz, 4) for dx in range(4) for dz in range(4)]
    for row in reversed(range(8)):
        for column in reversed(range(16)):
            if row or column:
                pl.semaphore_signal(
                    barrier, inc=1, device_id=(hxs[row], hys[column]), device_id_type=MESH
                )

    bucket_f = bucket_ref[...].astype(jnp.float32)
    bucket_cols = jnp.broadcast_to(bucket_f, (128, files)).T
    rank = jnp.zeros((1, files), jnp.float32)
    lane = lax.broadcasted_iota(jnp.int32, (128, files), 1)
    sub = lax.broadcasted_iota(jnp.int32, (128, files), 0)
    for block in range(files // 128):
        col = bucket_cols[block * 128 : (block + 1) * 128, 0:1]
        same = (col == bucket_f) & (sub + block * 128 < lane)
        rank = rank + jnp.sum(jnp.where(same, 1.0, 0.0), axis=0, keepdims=True)
    target = bucket_f * float(SLOTS) + rank
    slot_cols = jnp.broadcast_to(target, (128, files)).T

    def mixed(one, two):
        low = lax.broadcasted_iota(jnp.int32, one.shape, 1) < SLOTS
        first = jnp.where(low, one, pltpu.roll(two, SLOTS, 1))
        second = jnp.where(low, pltpu.roll(one, SLOTS, 1), two)
        return first, second

    def fold_rows(values):
        count = values.shape[0] // 8
        one, two = mixed(
            values[:, :half].reshape(count, 8, half), values[:, half:].reshape(count, 8, half)
        )
        return jnp.stack([one, two], axis=1).reshape(count * 2, 8, half).astype(jnp.bfloat16)

    def unfold_rows(packed):
        count = packed.shape[0] // 2
        halves = packed.astype(jnp.float32).reshape(count, 2, 8, half)
        first, second = mixed(halves[:, 0], halves[:, 1])
        return first.reshape(count * 8, half), second.reshape(count * 8, half)

    rows = rows_ref[...]

    def pack(block, carry):
        place = lax.broadcasted_iota(jnp.int32, (256, files), 0) + block * 256
        match = (place.astype(jnp.float32) == target).astype(jnp.float32)
        used = jnp.sum(match, axis=1, keepdims=True)
        packed = jnp.dot(match.astype(jnp.bfloat16), rows, preferred_element_type=jnp.float32)
        send_buf[pl.ds(block * 64, 64)] = fold_rows(jnp.where(used > 0.5, packed, EMPTY))
        return carry

    lax.fori_loop(0, BUCKETS * SLOTS // 256, pack, 0)

    pl.semaphore_wait(barrier, devices - 1)

    hy_low = [2 * rem(hy, 8) for hy in hys]
    hy_flip = [div(hy, 8) for hy in hys]
    cross = [(column // 4 + column) % 4 for column in range(16)]

    def send(y, column, core, slot):
        offset = OFFSET[DIRECT[core][slot]]
        pltpu.make_async_remote_copy(
            src_ref=send_buf.at[
                32 * y + hy_low[column] + offset + hy_flip[column] * (145 - 2 * offset)
            ],
            dst_ref=raw.at[slot, me],
            send_sem=send_sem.at[slot],
            recv_sem=recv_sem.at[slot],
            device_id=(y * 2 + core, hys[column]),
            device_id_type=MESH,
        ).start()

    def keep(core, slot):
        return pltpu.make_async_copy(
            send_buf.at[bucket_at(my_y, my_hy, DIRECT[core][slot])],
            raw.at[slot, me],
            local_sem.at[slot],
        )

    for core in range(2):

        @pl.when(my_core == core)
        def _():
            for slot in range(len(DIRECT[core])):
                keep(core, slot).start()
            for slot in range(len(DIRECT[1 - core])):
                send(my_y, 0, 1 - core, slot)

    def send_slot(slot, cores):
        def around(turn, carry):
            ys = [rem(my_y + turn + shift, 4) for shift in range(4)]
            for column in reversed(range(1, 16)):
                for core in cores:
                    send(ys[cross[column]], column, core, slot)

            @pl.when(turn > 0)
            def _():
                for core in cores:
                    send(ys[0], 0, core, slot)

            return carry

        lax.fori_loop(0, 4, around, 0)

    chips = devices // 2
    send_slot(0, (0, 1))
    send_slot(1, (0, 1))
    send_slot(2, (0, 1))
    send_slot(3, (1,))

    def wait_count(buf, count, sem):
        part = buf.at[pl.ds(0, count)]
        pltpu.make_async_copy(part, part, sem).wait()

    def wait_slot(slot):
        wait_count(raw.at[slot], devices - 1, recv_sem.at[slot])

    def share(slot, there, sem):
        return pltpu.make_async_remote_copy(
            src_ref=raw.at[slot],
            dst_ref=raw.at[there],
            send_sem=send_sem.at[sem],
            recv_sem=recv_sem.at[there],
            device_id=(my_y * 2 + 1 - my_core, my_hy),
            device_id_type=MESH,
        )

    def wait_shared(slot):
        wait_count(raw.at[slot], devices, recv_sem.at[slot])

    scale_fold = sharpness / width * math.log2(math.e)

    def settle(slot, with_query):
        def block_step(block, carry):
            first, second = unfold_rows(raw[slot, pl.ds(block * SPAN, SPAN)])
            start = pl.multiple_of(block * (SPAN * 4), SPAN * 4)
            square = jnp.sum(first * first + second * second, axis=1, keepdims=True)
            inverse = 1.0 / jnp.sqrt(square * (1.0 / width) + epsilon)
            used = first[:, 0:1] < 100.0
            wide = jnp.broadcast_to(jnp.where(used, inverse, -1.0), (SPAN * 4, 128))
            across = wide.T[0:1, :]
            keys[slot, pl.ds(start, SPAN * 4), 0:half] = first.astype(jnp.bfloat16)
            keys[slot, pl.ds(start, SPAN * 4), half:width] = second.astype(jnp.bfloat16)
            key_scale[slot, :, pl.ds(start, SPAN * 4)] = across
            key_bias[slot, :, pl.ds(start, SPAN * 4)] = jnp.where(across > 0.0, 0.0, FAR)
            if with_query:
                query_scale[slot, pl.ds(start, SPAN * 4), :] = jnp.broadcast_to(
                    inverse * scale_fold, (SPAN * 4, 128)
                )
            return carry

        lax.fori_loop(0, devices // SPAN, block_step, 0)

    def pair_tile(query, start, tile, key, skip_self):
        queries = keys[query, pl.ds(start, tile), :]
        against = keys[key]
        products = lax.dot_general(
            queries, against, (((1,), (1,)), ((), ())), preferred_element_type=jnp.float32
        )
        scale = query_scale[query, pl.ds(start, tile), :][:, 0:1]
        weight = jnp.exp2(products * scale * key_scale[key] + key_bias[key])
        if skip_self:
            row = lax.broadcasted_iota(jnp.int32, (tile, CAP), 0) + start
            col = lax.broadcasted_iota(jnp.int32, (tile, CAP), 1)
            weight = jnp.where(row == col, 0.0, weight)
        total = weight[:, 0:128]
        for part in range(1, CAP // 128):
            total = total + weight[:, part * 128 : (part + 1) * 128]
        summed = jnp.dot(weight.astype(jnp.bfloat16), against, preferred_element_type=jnp.float32)
        return summed, total

    def own_pair(query):
        summed, total = pair_tile(query, 0, CAP, query, True)
        numer[query] = summed
        denom[query] = total

    def pair(query, key):
        summed, total = pair_tile(query, 0, CAP, key, False)
        numer[query] += summed
        denom[query] += total

    def my_bucket(query):
        offset = query + my_core * (16 + 111 * query)
        return 32 * my_y + 2 * rem(my_hy, 8) + offset + div(my_hy, 8) * (145 - 2 * offset)

    def keep_back(query):
        return pltpu.make_async_copy(
            back_buf.at[query, me], home_buf.at[my_bucket(query)], local_sem.at[4 + query]
        )

    def finish(query, key):
        mine = my_bucket(query)

        def block_step(step, carry):
            upper = rem(div(my_y, 2) + 1 + step, 2)
            start = pl.multiple_of(upper * 256, 256)
            summed, total = pair_tile(query, start, 256, key, False)
            whole = numer[query, pl.ds(start, 256), :] + summed
            under = denom[query, pl.ds(start, 256), :] + total
            under = 1.0 + jnp.sum(under, axis=1, keepdims=True)
            back_buf[query, pl.ds(upper * 64, 64)] = fold_rows(whole * (1.0 / under))

            def give(turn, inner):
                y = 2 * upper + rem(my_y + 1 + turn, 2)
                for column in reversed(range(16)):
                    for core in range(2):
                        to = (y * 2 + core) * 16 + hys[column]

                        def start_copy():
                            pltpu.make_async_remote_copy(
                                src_ref=back_buf.at[query, to],
                                dst_ref=home_buf.at[mine],
                                send_sem=send_sem.at[7 + query],
                                recv_sem=recv_sem.at[6],
                                device_id=(y * 2 + core, hys[column]),
                                device_id_type=MESH,
                            ).start()

                        if column:
                            start_copy()
                        else:
                            pl.when(to != me)(start_copy)
                return inner

            lax.fori_loop(0, 2, give, 0)
            return carry

        lax.fori_loop(0, 2, block_step, 0)
        keep_back(query).start()

    wait_slot(0)
    keep(0, 0).wait()
    first_share = share(0, 4 - my_core, 4)
    first_share.start()
    settle(0, True)
    own_pair(0)
    given = 3 + my_core
    wait_shared(given)
    settle(given, False)
    pair(0, given)
    wait_slot(1)
    keep(0, 1).wait()

    @pl.when(my_core == 1)
    def _():
        share(1, 4, 5).start()

    settle(1, True)

    @pl.when(my_core == 0)
    def _():
        pair(0, 1)
        wait_shared(4)
        settle(4, False)
        finish(0, 4)

    own_pair(1)
    pair(1, 4 * my_core)
    wait_slot(2)
    keep(0, 2).wait()
    second_share = share(2, 5, 6)
    second_share.start()
    settle(2, False)
    pair(1 - my_core, 2)
    wait_shared(5)
    settle(5, False)

    @pl.when(my_core == 1)
    def _():
        pair(1, 5)
        wait_slot(3)
        keep(1, 3).wait()
        settle(3, False)

    def last(index, carry):
        finish(1 - my_core + index, 5 - 2 * my_core)
        return carry

    lax.fori_loop(0, 1 + my_core, last, 0)
    keep_back(0).wait()
    keep_back(1).wait()
    first_share.wait_send()
    second_share.wait_send()

    @pl.when(my_core == 1)
    def _():
        share(1, 4, 5).wait_send()

    got = home_buf.at[pl.ds(0, BUCKETS - 2)]
    pltpu.make_async_copy(got, got, recv_sem.at[6]).wait()

    slot_wide = jnp.concatenate([slot_cols, slot_cols], axis=1)
    place = lax.broadcasted_iota(jnp.int32, (files, 256), 1).astype(jnp.float32)
    results = [jnp.zeros((files, half), jnp.float32) for _ in range(2)]
    for block in range(BUCKETS * SLOTS // 256):
        match = (slot_wide == place + float(block * 256)).astype(jnp.float32).astype(jnp.bfloat16)
        parts = unfold_rows(home_buf[pl.ds(block * 64, 64)])
        results = [
            result + jnp.dot(match, part.astype(jnp.bfloat16), preferred_element_type=jnp.float32)
            for result, part in zip(results, parts)
        ]
    out_ref[:, 0:half] = results[0].astype(jnp.bfloat16)
    out_ref[:, half:width] = results[1].astype(jnp.bfloat16)

    for slot in range(3):
        wait_count(raw.at[slot], devices - 1, send_sem.at[slot])
    for core in range(2):

        @pl.when(my_core == core)
        def _():
            wait_count(raw.at[3], chips - core, send_sem.at[3])

    for query in range(2):
        wait_count(raw.at[query], devices - 1, send_sem.at[7 + query])


def solution(mesh):
    devices = mesh.shape["hx"] * mesh.shape["hy"]

    def body(embeddings, bucket):
        files, width = embeddings.shape
        half = width // 2
        return pl.pallas_call(
            kernel,
            out_shape=jax.ShapeDtypeStruct((files, width), jnp.bfloat16),
            in_specs=[pl.BlockSpec(memory_space=pltpu.VMEM)] * 2,
            out_specs=pl.BlockSpec(memory_space=pltpu.VMEM),
            scratch_shapes=[
                pltpu.VMEM((BUCKETS, 8, half), jnp.bfloat16),
                pltpu.VMEM((6, devices, 8, half), jnp.bfloat16),
                pltpu.VMEM((2, devices, 8, half), jnp.bfloat16),
                pltpu.VMEM((BUCKETS, 8, half), jnp.bfloat16),
                pltpu.VMEM((6, CAP, width), jnp.bfloat16),
                pltpu.VMEM((6, 1, CAP), jnp.float32),
                pltpu.VMEM((6, 1, CAP), jnp.float32),
                pltpu.VMEM((2, CAP, 128), jnp.float32),
                pltpu.VMEM((2, CAP, width), jnp.float32),
                pltpu.VMEM((2, CAP, 128), jnp.float32),
                pltpu.SemaphoreType.DMA((9,)),
                pltpu.SemaphoreType.DMA((7,)),
                pltpu.SemaphoreType.DMA((6,)),
            ],
            compiler_params=pltpu.CompilerParams(
                collective_id=0, has_side_effects=True, vmem_limit_bytes=60 * 1024 * 1024
            ),
        )(embeddings, bucket.reshape(1, files))

    return jax.shard_map(
        body,
        mesh=mesh,
        in_specs=(P(("hx", "hy"), None), P(("hx", "hy"))),
        out_specs=P(("hx", "hy"), None),
        check_vma=False,
    )
```

```python
import functools
import math

import jax
import jax.numpy as jnp
from jax import lax
from jax.experimental import pallas as pl
from jax.experimental.pallas import tpu as pltpu
from jax.sharding import PartitionSpec as P

MESH = pl.DeviceIdType.MESH

CAP = 512
BUCKETS = 256
SLOTS = 4
sharpness = 32.0
epsilon = 1e-06
EMPTY = 128.0
FAR = -1e30
SPAN = 64

OFFSET = {name: 128 * (name // 100) + 16 * (name // 10 % 10) + name % 10 for name in (0, 1, 10, 11, 100, 101, 110)}
DIRECT = ((0, 1, 101), (10, 100, 11, 110))


def rem(value, by):
    return lax.rem(value, jnp.int32(by))


def div(value, by):
    return lax.div(value, jnp.int32(by))


def apart(shift):
    return min(shift, 4 - shift)


def kernel(
    rows_hbm,
    bucket_hbm,
    out_ref,
    rows_ref,
    bucket_ref,
    send_buf,
    raw,
    back_buf,
    home_buf,
    keys,
    key_scale,
    key_bias,
    query_scale,
    numer,
    denom,
    send_sem,
    recv_sem,
    local_sem,
):
    files, width = rows_hbm.shape
    devices = raw.shape[1]
    half = width // 2
    my_hx = lax.axis_index("hx")
    my_hy = lax.axis_index("hy")
    my_core = rem(my_hx, 2)
    my_y = div(my_hx, 2)
    my_x = div(my_hy, 4)
    my_z = rem(my_hy, 4)
    me = my_hx * 16 + my_hy

    def bucket_at(y, hy, name):
        offset = OFFSET[name]
        return 32 * y + 2 * rem(hy, 8) + offset + div(hy, 8) * (145 - 2 * offset)

    barrier = pltpu.get_barrier_semaphore()
    hxs = [rem(my_y + dy, 4) * 2 + rem(my_core + core, 2) for dy in range(4) for core in range(2)]
    hys = [rem(my_x + dx, 4) * 4 + rem(my_z + dz, 4) for dx in range(4) for dz in range(4)]
    far_first = sorted(
        ((row, column) for row in range(8) for column in range(16) if row or column),
        key=lambda at: -(apart(at[0] // 2) + apart(at[1] // 4) + apart(at[1] % 4)),
    )
    for row, column in far_first:
        pl.semaphore_signal(
            barrier, inc=1, device_id=(hxs[row], hys[column]), device_id_type=MESH
        )
    fetch = pltpu.make_async_copy(rows_hbm, rows_ref, local_sem.at[6])
    fetch.start()
    fetch_bucket = pltpu.make_async_copy(bucket_hbm, bucket_ref, local_sem.at[7])
    fetch_bucket.start()
    fetch_bucket.wait()

    bucket_f = bucket_ref[...].astype(jnp.float32)
    bucket_cols = jnp.broadcast_to(bucket_f, (128, files)).T
    rank = jnp.zeros((1, files), jnp.float32)
    lane = lax.broadcasted_iota(jnp.int32, (128, files), 1)
    sub = lax.broadcasted_iota(jnp.int32, (128, files), 0)
    for block in range(files // 128):
        col = bucket_cols[block * 128 : (block + 1) * 128, 0:1]
        same = (col == bucket_f) & (sub + block * 128 < lane)
        rank = rank + jnp.sum(jnp.where(same, 1.0, 0.0), axis=0, keepdims=True)
    target = bucket_f * float(SLOTS) + rank
    slot_cols = jnp.broadcast_to(target, (128, files)).T

    def mixed(one, two):
        low = lax.broadcasted_iota(jnp.int32, one.shape, 1) < SLOTS
        first = jnp.where(low, one, pltpu.roll(two, SLOTS, 1))
        second = jnp.where(low, pltpu.roll(one, SLOTS, 1), two)
        return first, second

    def fold_rows(values):
        count = values.shape[0] // 8
        one, two = mixed(
            values[:, :half].reshape(count, 8, half), values[:, half:].reshape(count, 8, half)
        )
        return jnp.stack([one, two], axis=1).reshape(count * 2, 8, half).astype(jnp.bfloat16)

    def unfold_rows(packed):
        count = packed.shape[0] // 2
        halves = packed.astype(jnp.float32).reshape(count, 2, 8, half)
        first, second = mixed(halves[:, 0], halves[:, 1])
        return first.reshape(count * 8, half), second.reshape(count * 8, half)

    fetch.wait()
    rows = rows_ref[...]

    def pack(block, carry):
        place = lax.broadcasted_iota(jnp.int32, (256, files), 0) + block * 256
        match = (place.astype(jnp.float32) == target).astype(jnp.float32)
        used = jnp.sum(match, axis=1, keepdims=True)
        packed = jnp.dot(match.astype(jnp.bfloat16), rows, preferred_element_type=jnp.float32)
        send_buf[pl.ds(block * 64, 64)] = fold_rows(jnp.where(used > 0.5, packed, EMPTY))
        return carry

    lax.fori_loop(0, BUCKETS * SLOTS // 256, pack, 0)

    pl.semaphore_wait(barrier, devices - 1)

    hy_low = [2 * rem(hy, 8) for hy in hys]
    hy_flip = [div(hy, 8) for hy in hys]
    cross = [(column // 4 + column) % 4 for column in range(16)]

    def send(y, column, core, slot):
        offset = OFFSET[DIRECT[core][slot]]
        pltpu.make_async_remote_copy(
            src_ref=send_buf.at[
                32 * y + hy_low[column] + offset + hy_flip[column] * (145 - 2 * offset)
            ],
            dst_ref=raw.at[slot, me],
            send_sem=send_sem.at[slot],
            recv_sem=recv_sem.at[slot],
            device_id=(y * 2 + core, hys[column]),
            device_id_type=MESH,
        ).start()

    def keep(core, slot):
        return pltpu.make_async_copy(
            send_buf.at[bucket_at(my_y, my_hy, DIRECT[core][slot])],
            raw.at[slot, me],
            local_sem.at[slot],
        )

    for core in range(2):

        @pl.when(my_core == core)
        def _():
            for slot in range(len(DIRECT[core])):
                keep(core, slot).start()
            for slot in range(len(DIRECT[1 - core])):
                send(my_y, 0, 1 - core, slot)

    def send_slot(slot, cores):
        def around(turn, carry):
            ys = [rem(my_y + turn + shift, 4) for shift in range(4)]
            for column in reversed(range(1, 16)):
                for core in cores:
                    send(ys[cross[column]], column, core, slot)

            @pl.when(turn > 0)
            def _():
                for core in cores:
                    send(ys[0], 0, core, slot)

            return carry

        lax.fori_loop(0, 4, around, 0)

    chips = devices // 2
    send_slot(0, (0, 1))
    send_slot(1, (0, 1))
    send_slot(2, (0, 1))
    send_slot(3, (1,))

    def wait_count(buf, count, sem):
        part = buf.at[pl.ds(0, count)]
        pltpu.make_async_copy(part, part, sem).wait()

    def wait_slot(slot):
        wait_count(raw.at[slot], devices - 1, recv_sem.at[slot])

    def share(slot, there, sem):
        return pltpu.make_async_remote_copy(
            src_ref=raw.at[slot],
            dst_ref=raw.at[there],
            send_sem=send_sem.at[sem],
            recv_sem=recv_sem.at[there],
            device_id=(my_y * 2 + 1 - my_core, my_hy),
            device_id_type=MESH,
        )

    def wait_shared(slot):
        wait_count(raw.at[slot], devices, recv_sem.at[slot])

    scale_fold = sharpness / width * math.log2(math.e)

    def settle(slot, with_query):
        def block_step(block, carry):
            first, second = unfold_rows(raw[slot, pl.ds(block * SPAN, SPAN)])
            start = pl.multiple_of(block * (SPAN * 4), SPAN * 4)
            square = jnp.sum(first * first + second * second, axis=1, keepdims=True)
            inverse = 1.0 / jnp.sqrt(square * (1.0 / width) + epsilon)
            used = first[:, 0:1] < 100.0
            wide = jnp.broadcast_to(jnp.where(used, inverse, -1.0), (SPAN * 4, 128))
            across = wide.T[0:1, :]
            keys[slot, pl.ds(start, SPAN * 4), 0:half] = first.astype(jnp.bfloat16)
            keys[slot, pl.ds(start, SPAN * 4), half:width] = second.astype(jnp.bfloat16)
            key_scale[slot, :, pl.ds(start, SPAN * 4)] = across
            key_bias[slot, :, pl.ds(start, SPAN * 4)] = jnp.where(across > 0.0, 0.0, FAR)
            if with_query:
                query_scale[slot, pl.ds(start, SPAN * 4), :] = jnp.broadcast_to(
                    inverse * scale_fold, (SPAN * 4, 128)
                )
            return carry

        lax.fori_loop(0, devices // SPAN, block_step, 0)

    def pair_tile(query, start, tile, key, skip_self):
        queries = keys[query, pl.ds(start, tile), :]
        against = keys[key]
        products = lax.dot_general(
            queries, against, (((1,), (1,)), ((), ())), preferred_element_type=jnp.float32
        )
        scale = query_scale[query, pl.ds(start, tile), :][:, 0:1]
        weight = jnp.exp2(products * scale * key_scale[key] + key_bias[key])
        if skip_self:
            row = lax.broadcasted_iota(jnp.int32, (tile, CAP), 0) + start
            col = lax.broadcasted_iota(jnp.int32, (tile, CAP), 1)
            weight = jnp.where(row == col, 0.0, weight)
        total = weight[:, 0:128]
        for part in range(1, CAP // 128):
            total = total + weight[:, part * 128 : (part + 1) * 128]
        summed = jnp.dot(weight.astype(jnp.bfloat16), against, preferred_element_type=jnp.float32)
        return summed, total

    def own_pair(query):
        summed, total = pair_tile(query, 0, CAP, query, True)
        numer[query] = summed
        denom[query] = total

    def pair(query, key):
        summed, total = pair_tile(query, 0, CAP, key, False)
        numer[query] += summed
        denom[query] += total

    def my_bucket(query):
        offset = query + my_core * (16 + 111 * query)
        return 32 * my_y + 2 * rem(my_hy, 8) + offset + div(my_hy, 8) * (145 - 2 * offset)

    def keep_back(query):
        return pltpu.make_async_copy(
            back_buf.at[query, me], home_buf.at[my_bucket(query)], local_sem.at[4 + query]
        )

    def finish(query, key):
        mine = my_bucket(query)

        def block_step(step, carry):
            upper = rem(div(my_y, 2) + 1 + step, 2)
            start = pl.multiple_of(upper * 256, 256)
            summed, total = pair_tile(query, start, 256, key, False)
            whole = numer[query, pl.ds(start, 256), :] + summed
            under = denom[query, pl.ds(start, 256), :] + total
            under = 1.0 + jnp.sum(under, axis=1, keepdims=True)
            back_buf[query, pl.ds(upper * 64, 64)] = fold_rows(whole * (1.0 / under))

            def give(turn, inner):
                y = 2 * upper + rem(my_y + 1 + turn, 2)
                for column in reversed(range(16)):
                    for core in range(2):
                        to = (y * 2 + core) * 16 + hys[column]

                        def start_copy():
                            pltpu.make_async_remote_copy(
                                src_ref=back_buf.at[query, to],
                                dst_ref=home_buf.at[mine],
                                send_sem=send_sem.at[7 + query],
                                recv_sem=recv_sem.at[6],
                                device_id=(y * 2 + core, hys[column]),
                                device_id_type=MESH,
                            ).start()

                        if column:
                            start_copy()
                        else:
                            pl.when(to != me)(start_copy)
                return inner

            lax.fori_loop(0, 2, give, 0)
            return carry

        lax.fori_loop(0, 2, block_step, 0)
        keep_back(query).start()

    wait_slot(0)
    keep(0, 0).wait()
    first_share = share(0, 4 - my_core, 4)
    first_share.start()
    settle(0, True)
    own_pair(0)
    given = 3 + my_core
    wait_shared(given)
    settle(given, False)
    pair(0, given)
    wait_slot(1)
    keep(0, 1).wait()

    @pl.when(my_core == 1)
    def _():
        share(1, 4, 5).start()

    settle(1, True)

    @pl.when(my_core == 0)
    def _():
        pair(0, 1)
        wait_shared(4)
        settle(4, False)
        finish(0, 4)

    own_pair(1)
    pair(1, 4 * my_core)
    wait_slot(2)
    keep(0, 2).wait()
    second_share = share(2, 5, 6)
    second_share.start()
    settle(2, False)
    pair(1 - my_core, 2)
    wait_shared(5)
    settle(5, False)

    @pl.when(my_core == 1)
    def _():
        pair(1, 5)
        wait_slot(3)
        keep(1, 3).wait()
        settle(3, False)

    def last(index, carry):
        finish(1 - my_core + index, 5 - 2 * my_core)
        return carry

    lax.fori_loop(0, 1 + my_core, last, 0)
    keep_back(0).wait()
    keep_back(1).wait()
    first_share.wait_send()
    second_share.wait_send()

    @pl.when(my_core == 1)
    def _():
        share(1, 4, 5).wait_send()

    got = home_buf.at[pl.ds(0, BUCKETS - 2)]
    pltpu.make_async_copy(got, got, recv_sem.at[6]).wait()

    slot_wide = jnp.concatenate([slot_cols, slot_cols], axis=1)
    place = lax.broadcasted_iota(jnp.int32, (files, 256), 1).astype(jnp.float32)
    results = [jnp.zeros((files, half), jnp.float32) for _ in range(2)]
    for block in range(BUCKETS * SLOTS // 256):
        match = (slot_wide == place + float(block * 256)).astype(jnp.float32).astype(jnp.bfloat16)
        parts = unfold_rows(home_buf[pl.ds(block * 64, 64)])
        results = [
            result + jnp.dot(match, part.astype(jnp.bfloat16), preferred_element_type=jnp.float32)
            for result, part in zip(results, parts)
        ]
    out_ref[:, 0:half] = results[0].astype(jnp.bfloat16)
    out_ref[:, half:width] = results[1].astype(jnp.bfloat16)

    for slot in range(3):
        wait_count(raw.at[slot], devices - 1, send_sem.at[slot])
    for core in range(2):

        @pl.when(my_core == core)
        def _():
            wait_count(raw.at[3], chips - core, send_sem.at[3])

    for query in range(2):
        wait_count(raw.at[query], devices - 1, send_sem.at[7 + query])


def solution(mesh):
    devices = mesh.shape["hx"] * mesh.shape["hy"]

    def body(embeddings, bucket):
        files, width = embeddings.shape
        half = width // 2
        return pl.pallas_call(
            kernel,
            out_shape=jax.ShapeDtypeStruct((files, width), jnp.bfloat16),
            in_specs=[pl.BlockSpec(memory_space=pltpu.HBM)] * 2,
            out_specs=pl.BlockSpec(memory_space=pltpu.VMEM),
            scratch_shapes=[
                pltpu.VMEM((files, width), jnp.bfloat16),
                pltpu.VMEM((1, files), jnp.int32),
                pltpu.VMEM((BUCKETS, 8, half), jnp.bfloat16),
                pltpu.VMEM((6, devices, 8, half), jnp.bfloat16),
                pltpu.VMEM((2, devices, 8, half), jnp.bfloat16),
                pltpu.VMEM((BUCKETS, 8, half), jnp.bfloat16),
                pltpu.VMEM((6, CAP, width), jnp.bfloat16),
                pltpu.VMEM((6, 1, CAP), jnp.float32),
                pltpu.VMEM((6, 1, CAP), jnp.float32),
                pltpu.VMEM((2, CAP, 128), jnp.float32),
                pltpu.VMEM((2, CAP, width), jnp.float32),
                pltpu.VMEM((2, CAP, 128), jnp.float32),
                pltpu.SemaphoreType.DMA((9,)),
                pltpu.SemaphoreType.DMA((7,)),
                pltpu.SemaphoreType.DMA((8,)),
            ],
            compiler_params=pltpu.CompilerParams(
                collective_id=0, has_side_effects=True, vmem_limit_bytes=32 * 1024 * 1024
            ),
        )(
            pltpu.with_memory_space_constraint(embeddings, pltpu.HBM),
            pltpu.with_memory_space_constraint(bucket.reshape(1, files), pltpu.HBM),
        )

    return jax.shard_map(
        body,
        mesh=mesh,
        in_specs=(P(("hx", "hy"), None), P(("hx", "hy"))),
        out_specs=P(("hx", "hy"), None),
        check_vma=False,
    )
```

```python
import functools
import math

import jax
import jax.numpy as jnp
from jax import lax
from jax.experimental import pallas as pl
from jax.experimental.pallas import tpu as pltpu
from jax.sharding import PartitionSpec as P

MESH = pl.DeviceIdType.MESH

CAP = 512
BUCKETS = 256
SLOTS = 4
sharpness = 32.0
epsilon = 1e-06
EMPTY = 128.0
FAR = -1e30
SPAN = 64

OFFSET = {name: 128 * (name // 100) + 16 * (name // 10 % 10) + name % 10 for name in (0, 1, 10, 11, 100, 101, 110)}
DIRECT = ((0, 1, 101), (10, 100, 11, 110))


def rem(value, by):
    return lax.rem(value, jnp.int32(by))


def div(value, by):
    return lax.div(value, jnp.int32(by))


def apart(shift):
    return min(shift, 4 - shift)


def kernel(
    rows_hbm,
    bucket_hbm,
    out_ref,
    rows_ref,
    bucket_ref,
    send_buf,
    raw,
    back_buf,
    home_buf,
    keys,
    key_scale,
    key_bias,
    query_scale,
    numer,
    denom,
    send_sem,
    recv_sem,
    local_sem,
):
    files, width = rows_hbm.shape
    devices = raw.shape[1]
    half = width // 2
    my_hx = lax.axis_index("hx")
    my_hy = lax.axis_index("hy")
    my_core = rem(my_hx, 2)
    my_y = div(my_hx, 2)
    my_x = div(my_hy, 4)
    my_z = rem(my_hy, 4)
    me = my_hx * 16 + my_hy

    def bucket_at(y, hy, name):
        offset = OFFSET[name]
        return 32 * y + 2 * rem(hy, 8) + offset + div(hy, 8) * (145 - 2 * offset)

    fetch_bucket = pltpu.make_async_copy(bucket_hbm, bucket_ref, local_sem.at[7])
    fetch_bucket.start()
    fetch = pltpu.make_async_copy(rows_hbm, rows_ref, local_sem.at[6])
    fetch.start()
    barrier = pltpu.get_barrier_semaphore()
    hxs = [rem(my_y + dy, 4) * 2 + rem(my_core + core, 2) for dy in range(4) for core in range(2)]
    hys = [rem(my_x + dx, 4) * 4 + rem(my_z + dz, 4) for dx in range(4) for dz in range(4)]
    far_first = sorted(
        ((row, column) for row in range(8) for column in range(16) if row or column),
        key=lambda at: -(apart(at[0] // 2) + apart(at[1] // 4) + apart(at[1] % 4)),
    )
    for row, column in far_first:
        pl.semaphore_signal(
            barrier, inc=1, device_id=(hxs[row], hys[column]), device_id_type=MESH
        )
    fetch_bucket.wait()

    bucket_f = bucket_ref[...].astype(jnp.float32)
    bucket_cols = jnp.broadcast_to(bucket_f, (128, files)).T
    rank = jnp.zeros((1, files), jnp.float32)
    lane = lax.broadcasted_iota(jnp.int32, (128, files), 1)
    sub = lax.broadcasted_iota(jnp.int32, (128, files), 0)
    for block in range(files // 128):
        col = bucket_cols[block * 128 : (block + 1) * 128, 0:1]
        same = (col == bucket_f) & (sub + block * 128 < lane)
        rank = rank + jnp.sum(jnp.where(same, 1.0, 0.0), axis=0, keepdims=True)
    target = bucket_f * float(SLOTS) + rank
    slot_cols = jnp.broadcast_to(target, (128, files)).T

    def mixed(one, two):
        low = lax.broadcasted_iota(jnp.int32, one.shape, 1) < SLOTS
        first = jnp.where(low, one, pltpu.roll(two, SLOTS, 1))
        second = jnp.where(low, pltpu.roll(one, SLOTS, 1), two)
        return first, second

    def fold_rows(values):
        count = values.shape[0] // 8
        one, two = mixed(
            values[:, :half].reshape(count, 8, half), values[:, half:].reshape(count, 8, half)
        )
        return jnp.stack([one, two], axis=1).reshape(count * 2, 8, half).astype(jnp.bfloat16)

    def unfold_rows(packed):
        count = packed.shape[0] // 2
        halves = packed.astype(jnp.float32).reshape(count, 2, 8, half)
        first, second = mixed(halves[:, 0], halves[:, 1])
        return first.reshape(count * 8, half), second.reshape(count * 8, half)

    fetch.wait()
    rows = rows_ref[...]

    def pack(block, carry):
        place = lax.broadcasted_iota(jnp.int32, (256, files), 0) + block * 256
        match = (place.astype(jnp.float32) == target).astype(jnp.float32)
        used = jnp.sum(match, axis=1, keepdims=True)
        packed = jnp.dot(match.astype(jnp.bfloat16), rows, preferred_element_type=jnp.float32)
        send_buf[pl.ds(block * 64, 64)] = fold_rows(jnp.where(used > 0.5, packed, EMPTY))
        return carry

    lax.fori_loop(0, BUCKETS * SLOTS // 256, pack, 0)

    pl.semaphore_wait(barrier, devices - 1)

    hy_low = [2 * rem(hy, 8) for hy in hys]
    hy_flip = [div(hy, 8) for hy in hys]
    cross = [(column // 4 + column) % 4 for column in range(16)]

    def send(y, column, core, slot):
        offset = OFFSET[DIRECT[core][slot]]
        pltpu.make_async_remote_copy(
            src_ref=send_buf.at[
                32 * y + hy_low[column] + offset + hy_flip[column] * (145 - 2 * offset)
            ],
            dst_ref=raw.at[slot, me],
            send_sem=send_sem.at[slot],
            recv_sem=recv_sem.at[slot],
            device_id=(y * 2 + core, hys[column]),
            device_id_type=MESH,
        ).start()

    def keep(core, slot):
        return pltpu.make_async_copy(
            send_buf.at[bucket_at(my_y, my_hy, DIRECT[core][slot])],
            raw.at[slot, me],
            local_sem.at[slot],
        )

    for core in range(2):

        @pl.when(my_core == core)
        def _():
            for slot in range(len(DIRECT[core])):
                keep(core, slot).start()
            for slot in range(len(DIRECT[1 - core])):
                send(my_y, 0, 1 - core, slot)

    def send_slot(slot, cores):
        def around(turn, carry):
            ys = [rem(my_y + turn + shift, 4) for shift in range(4)]
            for column in reversed(range(1, 16)):
                for core in cores:
                    send(ys[cross[column]], column, core, slot)

            @pl.when(turn > 0)
            def _():
                for core in cores:
                    send(ys[0], 0, core, slot)

            return carry

        lax.fori_loop(0, 4, around, 0)

    chips = devices // 2
    send_slot(0, (0, 1))
    send_slot(1, (0, 1))
    send_slot(2, (0, 1))
    send_slot(3, (1,))

    def wait_count(buf, count, sem):
        part = buf.at[pl.ds(0, count)]
        pltpu.make_async_copy(part, part, sem).wait()

    def wait_slot(slot):
        wait_count(raw.at[slot], devices - 1, recv_sem.at[slot])

    def share(slot, there, sem):
        return pltpu.make_async_remote_copy(
            src_ref=raw.at[slot],
            dst_ref=raw.at[there],
            send_sem=send_sem.at[sem],
            recv_sem=recv_sem.at[there],
            device_id=(my_y * 2 + 1 - my_core, my_hy),
            device_id_type=MESH,
        )

    def wait_shared(slot):
        wait_count(raw.at[slot], devices, recv_sem.at[slot])

    scale_fold = sharpness / width * math.log2(math.e)

    def settle(slot, with_query):
        def block_step(block, carry):
            first, second = unfold_rows(raw[slot, pl.ds(block * SPAN, SPAN)])
            start = pl.multiple_of(block * (SPAN * 4), SPAN * 4)
            square = jnp.sum(first * first + second * second, axis=1, keepdims=True)
            inverse = 1.0 / jnp.sqrt(square * (1.0 / width) + epsilon)
            used = first[:, 0:1] < 100.0
            wide = jnp.broadcast_to(jnp.where(used, inverse, -1.0), (SPAN * 4, 128))
            across = wide.T[0:1, :]
            keys[slot, pl.ds(start, SPAN * 4), 0:half] = first.astype(jnp.bfloat16)
            keys[slot, pl.ds(start, SPAN * 4), half:width] = second.astype(jnp.bfloat16)
            key_scale[slot, :, pl.ds(start, SPAN * 4)] = across
            key_bias[slot, :, pl.ds(start, SPAN * 4)] = jnp.where(across > 0.0, 0.0, FAR)
            if with_query:
                query_scale[slot, pl.ds(start, SPAN * 4), :] = jnp.broadcast_to(
                    inverse * scale_fold, (SPAN * 4, 128)
                )
            return carry

        lax.fori_loop(0, devices // SPAN, block_step, 0)

    def pair_tile(query, start, tile, key, skip_self):
        queries = keys[query, pl.ds(start, tile), :]
        against = keys[key]
        products = lax.dot_general(
            queries, against, (((1,), (1,)), ((), ())), preferred_element_type=jnp.float32
        )
        scale = query_scale[query, pl.ds(start, tile), :][:, 0:1]
        weight = jnp.exp2(products * scale * key_scale[key] + key_bias[key])
        if skip_self:
            row = lax.broadcasted_iota(jnp.int32, (tile, CAP), 0) + start
            col = lax.broadcasted_iota(jnp.int32, (tile, CAP), 1)
            weight = jnp.where(row == col, 0.0, weight)
        total = weight[:, 0:128]
        for part in range(1, CAP // 128):
            total = total + weight[:, part * 128 : (part + 1) * 128]
        summed = jnp.dot(weight.astype(jnp.bfloat16), against, preferred_element_type=jnp.float32)
        return summed, total

    def own_pair(query):
        summed, total = pair_tile(query, 0, CAP, query, True)
        numer[query] = summed
        denom[query] = total

    def pair(query, key):
        summed, total = pair_tile(query, 0, CAP, key, False)
        numer[query] += summed
        denom[query] += total

    def my_bucket(query):
        offset = query + my_core * (16 + 111 * query)
        return 32 * my_y + 2 * rem(my_hy, 8) + offset + div(my_hy, 8) * (145 - 2 * offset)

    def keep_back(query):
        return pltpu.make_async_copy(
            back_buf.at[query, me], home_buf.at[my_bucket(query)], local_sem.at[4 + query]
        )

    def finish(query, key):
        mine = my_bucket(query)

        def block_step(step, carry):
            upper = rem(div(my_y, 2) + 1 + step, 2)
            start = pl.multiple_of(upper * 256, 256)
            summed, total = pair_tile(query, start, 256, key, False)
            whole = numer[query, pl.ds(start, 256), :] + summed
            under = denom[query, pl.ds(start, 256), :] + total
            under = 1.0 + jnp.sum(under, axis=1, keepdims=True)
            back_buf[query, pl.ds(upper * 64, 64)] = fold_rows(whole * (1.0 / under))

            def give(turn, inner):
                y = 2 * upper + rem(my_y + 1 + turn, 2)
                for column in reversed(range(16)):
                    for core in range(2):
                        to = (y * 2 + core) * 16 + hys[column]

                        def start_copy():
                            pltpu.make_async_remote_copy(
                                src_ref=back_buf.at[query, to],
                                dst_ref=home_buf.at[mine],
                                send_sem=send_sem.at[7 + query],
                                recv_sem=recv_sem.at[6],
                                device_id=(y * 2 + core, hys[column]),
                                device_id_type=MESH,
                            ).start()

                        if column:
                            start_copy()
                        else:
                            pl.when(to != me)(start_copy)
                return inner

            lax.fori_loop(0, 2, give, 0)
            return carry

        lax.fori_loop(0, 2, block_step, 0)
        keep_back(query).start()

    wait_slot(0)
    keep(0, 0).wait()
    first_share = share(0, 4 - my_core, 4)
    first_share.start()
    settle(0, True)
    own_pair(0)
    given = 3 + my_core
    wait_shared(given)
    settle(given, False)
    pair(0, given)
    wait_slot(1)
    keep(0, 1).wait()

    @pl.when(my_core == 1)
    def _():
        share(1, 4, 5).start()

    settle(1, True)

    @pl.when(my_core == 0)
    def _():
        pair(0, 1)
        wait_shared(4)
        settle(4, False)
        finish(0, 4)

    own_pair(1)
    pair(1, 4 * my_core)
    wait_slot(2)
    keep(0, 2).wait()
    second_share = share(2, 5, 6)
    second_share.start()
    settle(2, False)
    pair(1 - my_core, 2)
    wait_shared(5)
    settle(5, False)

    @pl.when(my_core == 1)
    def _():
        pair(1, 5)
        wait_slot(3)
        keep(1, 3).wait()
        settle(3, False)

    def last(index, carry):
        finish(1 - my_core + index, 5 - 2 * my_core)
        return carry

    lax.fori_loop(0, 1 + my_core, last, 0)
    keep_back(0).wait()
    keep_back(1).wait()
    first_share.wait_send()
    second_share.wait_send()

    @pl.when(my_core == 1)
    def _():
        share(1, 4, 5).wait_send()

    got = home_buf.at[pl.ds(0, BUCKETS - 2)]
    pltpu.make_async_copy(got, got, recv_sem.at[6]).wait()

    slot_wide = jnp.concatenate([slot_cols, slot_cols], axis=1)
    place = lax.broadcasted_iota(jnp.int32, (files, 256), 1).astype(jnp.float32)
    results = [jnp.zeros((files, half), jnp.float32) for _ in range(2)]
    for block in range(BUCKETS * SLOTS // 256):
        match = (slot_wide == place + float(block * 256)).astype(jnp.float32).astype(jnp.bfloat16)
        parts = unfold_rows(home_buf[pl.ds(block * 64, 64)])
        results = [
            result + jnp.dot(match, part.astype(jnp.bfloat16), preferred_element_type=jnp.float32)
            for result, part in zip(results, parts)
        ]
    out_ref[:, 0:half] = results[0].astype(jnp.bfloat16)
    out_ref[:, half:width] = results[1].astype(jnp.bfloat16)

    for slot in range(3):
        wait_count(raw.at[slot], devices - 1, send_sem.at[slot])
    for core in range(2):

        @pl.when(my_core == core)
        def _():
            wait_count(raw.at[3], chips - core, send_sem.at[3])

    for query in range(2):
        wait_count(raw.at[query], devices - 1, send_sem.at[7 + query])


def solution(mesh):
    devices = mesh.shape["hx"] * mesh.shape["hy"]

    def body(embeddings, bucket):
        files, width = embeddings.shape
        half = width // 2
        return pl.pallas_call(
            kernel,
            out_shape=jax.ShapeDtypeStruct((files, width), jnp.bfloat16),
            in_specs=[pl.BlockSpec(memory_space=pltpu.HBM)] * 2,
            out_specs=pl.BlockSpec(memory_space=pltpu.VMEM),
            scratch_shapes=[
                pltpu.VMEM((files, width), jnp.bfloat16),
                pltpu.VMEM((1, files), jnp.int32),
                pltpu.VMEM((BUCKETS, 8, half), jnp.bfloat16),
                pltpu.VMEM((6, devices, 8, half), jnp.bfloat16),
                pltpu.VMEM((2, devices, 8, half), jnp.bfloat16),
                pltpu.VMEM((BUCKETS, 8, half), jnp.bfloat16),
                pltpu.VMEM((6, CAP, width), jnp.bfloat16),
                pltpu.VMEM((6, 1, CAP), jnp.float32),
                pltpu.VMEM((6, 1, CAP), jnp.float32),
                pltpu.VMEM((2, CAP, 128), jnp.float32),
                pltpu.VMEM((2, CAP, width), jnp.float32),
                pltpu.VMEM((2, CAP, 128), jnp.float32),
                pltpu.SemaphoreType.DMA((9,)),
                pltpu.SemaphoreType.DMA((7,)),
                pltpu.SemaphoreType.DMA((8,)),
            ],
            compiler_params=pltpu.CompilerParams(
                collective_id=0, has_side_effects=True, vmem_limit_bytes=32 * 1024 * 1024
            ),
        )(
            pltpu.with_memory_space_constraint(embeddings, pltpu.HBM),
            pltpu.with_memory_space_constraint(bucket.reshape(1, files), pltpu.HBM),
        )

    return jax.shard_map(
        body,
        mesh=mesh,
        in_specs=(P(("hx", "hy"), None), P(("hx", "hy"))),
        out_specs=P(("hx", "hy"), None),
        check_vma=False,
    )
```

```python
import functools
import math

import jax
import jax.numpy as jnp
from jax import lax
from jax.experimental import pallas as pl
from jax.experimental.pallas import tpu as pltpu
from jax.sharding import PartitionSpec as P

MESH = pl.DeviceIdType.MESH

CAP = 512
BUCKETS = 256
SLOTS = 4
sharpness = 32.0
epsilon = 1e-06
EMPTY = 128.0
FAR = -1e30
SPAN = 64

OFFSET = {name: 128 * (name // 100) + 16 * (name // 10 % 10) + name % 10 for name in (0, 1, 10, 11, 100, 101, 110)}
DIRECT = ((0, 1, 101), (10, 100, 11, 110))


def rem(value, by):
    return lax.rem(value, jnp.int32(by))


def div(value, by):
    return lax.div(value, jnp.int32(by))


def apart(shift):
    return min(shift, 4 - shift)


def kernel(
    rows_hbm,
    bucket_hbm,
    out_ref,
    rows_ref,
    bucket_ref,
    send_buf,
    raw,
    back_buf,
    home_buf,
    match_buf,
    keys,
    key_scale,
    key_bias,
    query_scale,
    numer,
    denom,
    send_sem,
    recv_sem,
    local_sem,
):
    files, width = rows_hbm.shape
    devices = raw.shape[1]
    half = width // 2
    my_hx = lax.axis_index("hx")
    my_hy = lax.axis_index("hy")
    my_core = rem(my_hx, 2)
    my_y = div(my_hx, 2)
    my_x = div(my_hy, 4)
    my_z = rem(my_hy, 4)
    me = my_hx * 16 + my_hy

    def bucket_at(y, hy, name):
        offset = OFFSET[name]
        return 32 * y + 2 * rem(hy, 8) + offset + div(hy, 8) * (145 - 2 * offset)

    fetch_bucket = pltpu.make_async_copy(bucket_hbm, bucket_ref, local_sem.at[7])
    fetch_bucket.start()
    fetch = pltpu.make_async_copy(rows_hbm, rows_ref, local_sem.at[6])
    fetch.start()
    barrier = pltpu.get_barrier_semaphore()
    hxs = [rem(my_y + dy, 4) * 2 + rem(my_core + core, 2) for dy in range(4) for core in range(2)]
    hys = [rem(my_x + dx, 4) * 4 + rem(my_z + dz, 4) for dx in range(4) for dz in range(4)]
    far_first = sorted(
        ((row, column) for row in range(8) for column in range(16) if row or column),
        key=lambda at: -(apart(at[0] // 2) + apart(at[1] // 4) + apart(at[1] % 4)),
    )
    for row, column in far_first:
        pl.semaphore_signal(
            barrier, inc=1, device_id=(hxs[row], hys[column]), device_id_type=MESH
        )
    fetch_bucket.wait()

    bucket_f = bucket_ref[...].astype(jnp.float32)
    bucket_cols = jnp.broadcast_to(bucket_f, (128, files)).T
    rank = jnp.zeros((1, files), jnp.float32)
    lane = lax.broadcasted_iota(jnp.int32, (128, files), 1)
    sub = lax.broadcasted_iota(jnp.int32, (128, files), 0)
    for block in range(files // 128):
        col = bucket_cols[block * 128 : (block + 1) * 128, 0:1]
        same = (col == bucket_f) & (sub + block * 128 < lane)
        rank = rank + jnp.sum(jnp.where(same, 1.0, 0.0), axis=0, keepdims=True)
    target = bucket_f * float(SLOTS) + rank

    def mixed(one, two):
        low = lax.broadcasted_iota(jnp.int32, one.shape, 1) < SLOTS
        first = jnp.where(low, one, pltpu.roll(two, SLOTS, 1))
        second = jnp.where(low, pltpu.roll(one, SLOTS, 1), two)
        return first, second

    def fold_rows(values):
        count = values.shape[0] // 8
        one, two = mixed(
            values[:, :half].reshape(count, 8, half), values[:, half:].reshape(count, 8, half)
        )
        return jnp.stack([one, two], axis=1).reshape(count * 2, 8, half).astype(jnp.bfloat16)

    def unfold_rows(packed):
        count = packed.shape[0] // 2
        halves = packed.astype(jnp.float32).reshape(count, 2, 8, half)
        first, second = mixed(halves[:, 0], halves[:, 1])
        return first.reshape(count * 8, half), second.reshape(count * 8, half)

    fetch.wait()
    rows = rows_ref[...]

    def pack(block, carry):
        place = lax.broadcasted_iota(jnp.int32, (256, files), 0) + block * 256
        match = (place.astype(jnp.float32) == target).astype(jnp.float32)
        used = jnp.sum(match, axis=1, keepdims=True)
        packed = jnp.dot(match.astype(jnp.bfloat16), rows, preferred_element_type=jnp.float32)
        send_buf[pl.ds(block * 64, 64)] = fold_rows(jnp.where(used > 0.5, packed, EMPTY))
        return carry

    lax.fori_loop(0, BUCKETS * SLOTS // 256, pack, 0)

    pl.semaphore_wait(barrier, devices - 1)

    hy_low = [2 * rem(hy, 8) for hy in hys]
    hy_flip = [div(hy, 8) for hy in hys]
    cross = [(column // 4 + column) % 4 for column in range(16)]

    def send(y, column, core, slot):
        offset = OFFSET[DIRECT[core][slot]]
        pltpu.make_async_remote_copy(
            src_ref=send_buf.at[
                32 * y + hy_low[column] + offset + hy_flip[column] * (145 - 2 * offset)
            ],
            dst_ref=raw.at[slot, me],
            send_sem=send_sem.at[slot],
            recv_sem=recv_sem.at[slot],
            device_id=(y * 2 + core, hys[column]),
            device_id_type=MESH,
        ).start()

    def keep(core, slot):
        return pltpu.make_async_copy(
            send_buf.at[bucket_at(my_y, my_hy, DIRECT[core][slot])],
            raw.at[slot, me],
            local_sem.at[slot],
        )

    for core in range(2):

        @pl.when(my_core == core)
        def _():
            for slot in range(len(DIRECT[core])):
                keep(core, slot).start()
            for slot in range(len(DIRECT[1 - core])):
                send(my_y, 0, 1 - core, slot)

    def send_slot(slot, cores):
        def around(turn, carry):
            ys = [rem(my_y + turn + shift, 4) for shift in range(4)]
            for column in reversed(range(1, 16)):
                for core in cores:
                    send(ys[cross[column]], column, core, slot)

            @pl.when(turn > 0)
            def _():
                for core in cores:
                    send(ys[0], 0, core, slot)

            return carry

        lax.fori_loop(0, 4, around, 0)

    chips = devices // 2
    send_slot(0, (0, 1))
    send_slot(1, (0, 1))
    send_slot(2, (0, 1))
    send_slot(3, (1,))

    number = bucket_ref[...]
    high, mid, least = (number // place % 2 for place in (128, 16, 1))
    flip = (high + mid + least) // 2
    section = (
        3 * (high + flip - 2 * high * flip)
        + 2 * (mid + flip - 2 * mid * flip)
        + (least + flip - 2 * least * flip)
    )
    chip_of = number // 32 % 4 * 16 + flip * 8 + number // 2 % 8
    home_row = ((section * chips + chip_of) * SLOTS).astype(jnp.float32) + rank
    slot_cols = jnp.broadcast_to(home_row, (128, files)).T
    slot_wide = jnp.concatenate([slot_cols, slot_cols], axis=1)
    place = lax.broadcasted_iota(jnp.int32, (files, 256), 1).astype(jnp.float32)
    for block in range(4):
        match = (slot_wide == place + float(block * 256)).astype(jnp.float32)
        match_buf[block] = match.astype(jnp.bfloat16)

    def wait_count(buf, count, sem):
        part = buf.at[pl.ds(0, count)]
        pltpu.make_async_copy(part, part, sem).wait()

    def wait_slot(slot):
        wait_count(raw.at[slot], devices - 1, recv_sem.at[slot])

    def share(slot, there, sem):
        return pltpu.make_async_remote_copy(
            src_ref=raw.at[slot],
            dst_ref=raw.at[there],
            send_sem=send_sem.at[sem],
            recv_sem=recv_sem.at[there],
            device_id=(my_y * 2 + 1 - my_core, my_hy),
            device_id_type=MESH,
        )

    def wait_shared(slot):
        wait_count(raw.at[slot], devices, recv_sem.at[slot])

    scale_fold = sharpness / width * math.log2(math.e)

    def settle(slot, with_query):
        def block_step(block, carry):
            first, second = unfold_rows(raw[slot, pl.ds(block * SPAN, SPAN)])
            start = pl.multiple_of(block * (SPAN * 4), SPAN * 4)
            square = jnp.sum(first * first + second * second, axis=1, keepdims=True)
            inverse = 1.0 / jnp.sqrt(square * (1.0 / width) + epsilon)
            used = first[:, 0:1] < 100.0
            wide = jnp.broadcast_to(jnp.where(used, inverse, -1.0), (SPAN * 4, 128))
            across = wide.T[0:1, :]
            keys[slot, pl.ds(start, SPAN * 4), 0:half] = first.astype(jnp.bfloat16)
            keys[slot, pl.ds(start, SPAN * 4), half:width] = second.astype(jnp.bfloat16)
            key_scale[slot, :, pl.ds(start, SPAN * 4)] = across
            key_bias[slot, :, pl.ds(start, SPAN * 4)] = jnp.where(across > 0.0, 0.0, FAR)
            if with_query:
                query_scale[slot, pl.ds(start, SPAN * 4), :] = jnp.broadcast_to(
                    inverse * scale_fold, (SPAN * 4, 128)
                )
            return carry

        lax.fori_loop(0, devices // SPAN, block_step, 0)

    def pair_tile(query, start, tile, key, skip_self):
        queries = keys[query, pl.ds(start, tile), :]
        against = keys[key]
        products = lax.dot_general(
            queries, against, (((1,), (1,)), ((), ())), preferred_element_type=jnp.float32
        )
        scale = query_scale[query, pl.ds(start, tile), :][:, 0:1]
        weight = jnp.exp2(products * scale * key_scale[key] + key_bias[key])
        if skip_self:
            row = lax.broadcasted_iota(jnp.int32, (tile, CAP), 0) + start
            col = lax.broadcasted_iota(jnp.int32, (tile, CAP), 1)
            weight = jnp.where(row == col, 0.0, weight)
        total = weight[:, 0:128]
        for part in range(1, CAP // 128):
            total = total + weight[:, part * 128 : (part + 1) * 128]
        summed = jnp.dot(weight.astype(jnp.bfloat16), against, preferred_element_type=jnp.float32)
        return summed, total

    def own_pair(query):
        summed, total = pair_tile(query, 0, CAP, query, True)
        numer[query] = summed
        denom[query] = total

    def pair(query, key):
        summed, total = pair_tile(query, 0, CAP, key, False)
        numer[query] += summed
        denom[query] += total

    def keep_back(query):
        return pltpu.make_async_copy(
            back_buf.at[query, me],
            home_buf.at[2 * my_core + query, my_y * 16 + my_hy],
            local_sem.at[4 + query],
        )

    def finish(query, key):
        mine = 2 * my_core + query

        def block_step(step, carry):
            upper = rem(div(my_y, 2) + 1 + step, 2)
            start = pl.multiple_of(upper * 256, 256)
            summed, total = pair_tile(query, start, 256, key, False)
            whole = numer[query, pl.ds(start, 256), :] + summed
            under = denom[query, pl.ds(start, 256), :] + total
            under = 1.0 + jnp.sum(under, axis=1, keepdims=True)
            back_buf[query, pl.ds(upper * 64, 64)] = fold_rows(whole * (1.0 / under))

            def give(turn, inner):
                y = 2 * upper + rem(my_y + 1 + turn, 2)
                for column in reversed(range(16)):
                    for core in range(2):
                        to = (y * 2 + core) * 16 + hys[column]

                        def start_copy():
                            pltpu.make_async_remote_copy(
                                src_ref=back_buf.at[query, to],
                                dst_ref=home_buf.at[mine, my_y * 16 + my_hy],
                                send_sem=send_sem.at[7 + query],
                                recv_sem=recv_sem.at[6 + mine],
                                device_id=(y * 2 + core, hys[column]),
                                device_id_type=MESH,
                            ).start()

                        if column:
                            start_copy()
                        else:
                            pl.when(to != me)(start_copy)
                return inner

            lax.fori_loop(0, 2, give, 0)
            return carry

        lax.fori_loop(0, 2, block_step, 0)
        keep_back(query).start()

    wait_slot(0)
    keep(0, 0).wait()
    first_share = share(0, 4 - my_core, 4)
    first_share.start()
    settle(0, True)
    own_pair(0)
    given = 3 + my_core
    wait_shared(given)
    settle(given, False)
    pair(0, given)
    wait_slot(1)
    keep(0, 1).wait()

    @pl.when(my_core == 1)
    def _():
        share(1, 4, 5).start()

    settle(1, True)

    @pl.when(my_core == 0)
    def _():
        pair(0, 1)
        wait_shared(4)
        settle(4, False)
        finish(0, 4)

    own_pair(1)
    pair(1, 4 * my_core)
    wait_slot(2)
    keep(0, 2).wait()
    second_share = share(2, 5, 6)
    second_share.start()
    settle(2, False)
    pair(1 - my_core, 2)
    wait_shared(5)
    settle(5, False)

    @pl.when(my_core == 1)
    def _():
        pair(1, 5)
        wait_slot(3)
        keep(1, 3).wait()
        settle(3, False)

    def last(index, carry):
        finish(1 - my_core + index, 5 - 2 * my_core)
        return carry

    lax.fori_loop(0, 1 + my_core, last, 0)
    keep_back(0).wait()
    keep_back(1).wait()
    first_share.wait_send()
    second_share.wait_send()

    @pl.when(my_core == 1)
    def _():
        share(1, 4, 5).wait_send()

    results = [0.0, 0.0]
    for block in range(4):
        for core in range(2):

            @pl.when(my_core == core)
            def _():
                count = chips - 1 if block // 2 == core else chips
                wait_count(home_buf.at[block], count, recv_sem.at[6 + block])

        parts = unfold_rows(home_buf[block])
        results = [
            result
            + jnp.dot(match_buf[block], part.astype(jnp.bfloat16), preferred_element_type=jnp.float32)
            for result, part in zip(results, parts)
        ]
    out_ref[:, 0:half] = results[0].astype(jnp.bfloat16)
    out_ref[:, half:width] = results[1].astype(jnp.bfloat16)

    for slot in range(3):
        wait_count(raw.at[slot], devices - 1, send_sem.at[slot])
    for core in range(2):

        @pl.when(my_core == core)
        def _():
            wait_count(raw.at[3], chips - core, send_sem.at[3])

    for query in range(2):
        wait_count(raw.at[query], devices - 1, send_sem.at[7 + query])


def solution(mesh):
    devices = mesh.shape["hx"] * mesh.shape["hy"]

    def body(embeddings, bucket):
        files, width = embeddings.shape
        half = width // 2
        return pl.pallas_call(
            kernel,
            out_shape=jax.ShapeDtypeStruct((files, width), jnp.bfloat16),
            in_specs=[pl.BlockSpec(memory_space=pltpu.HBM)] * 2,
            out_specs=pl.BlockSpec(memory_space=pltpu.VMEM),
            scratch_shapes=[
                pltpu.VMEM((files, width), jnp.bfloat16),
                pltpu.VMEM((1, files), jnp.int32),
                pltpu.VMEM((BUCKETS, 8, half), jnp.bfloat16),
                pltpu.VMEM((6, devices, 8, half), jnp.bfloat16),
                pltpu.VMEM((2, devices, 8, half), jnp.bfloat16),
                pltpu.VMEM((4, devices // 2, 8, half), jnp.bfloat16),
                pltpu.VMEM((4, files, 256), jnp.bfloat16),
                pltpu.VMEM((6, CAP, width), jnp.bfloat16),
                pltpu.VMEM((6, 1, CAP), jnp.float32),
                pltpu.VMEM((6, 1, CAP), jnp.float32),
                pltpu.VMEM((2, CAP, 128), jnp.float32),
                pltpu.VMEM((2, CAP, width), jnp.float32),
                pltpu.VMEM((2, CAP, 128), jnp.float32),
                pltpu.SemaphoreType.DMA((9,)),
                pltpu.SemaphoreType.DMA((10,)),
                pltpu.SemaphoreType.DMA((8,)),
            ],
            compiler_params=pltpu.CompilerParams(
                collective_id=0, has_side_effects=True, vmem_limit_bytes=32 * 1024 * 1024
            ),
        )(
            pltpu.with_memory_space_constraint(embeddings, pltpu.HBM),
            pltpu.with_memory_space_constraint(bucket.reshape(1, files), pltpu.HBM),
        )

    return jax.shard_map(
        body,
        mesh=mesh,
        in_specs=(P(("hx", "hy"), None), P(("hx", "hy"))),
        out_specs=P(("hx", "hy"), None),
        check_vma=False,
    )
```

```python
import functools
import math

import jax
import jax.numpy as jnp
from jax import lax
from jax.experimental import pallas as pl
from jax.experimental.pallas import tpu as pltpu
from jax.sharding import PartitionSpec as P

MESH = pl.DeviceIdType.MESH

CAP = 512
BUCKETS = 256
SLOTS = 4
sharpness = 32.0
epsilon = 1e-06
EMPTY = 128.0
FAR = -1e30
SPAN = 64
MIXED = [at % 4 * 4 + (at // 4 + at) % 4 for at in range(16)]

OFFSET = {name: 128 * (name // 100) + 16 * (name // 10 % 10) + name % 10 for name in (0, 1, 10, 11, 100, 101, 110)}
DIRECT = ((0, 1, 101), (10, 100, 11, 110))


def rem(value, by):
    return lax.rem(value, jnp.int32(by))


def div(value, by):
    return lax.div(value, jnp.int32(by))


def apart(shift):
    return min(shift, 4 - shift)


def kernel(
    rows_hbm,
    bucket_hbm,
    out_ref,
    rows_ref,
    bucket_ref,
    send_buf,
    raw,
    back_buf,
    home_buf,
    match_buf,
    keys,
    key_scale,
    key_bias,
    query_scale,
    numer,
    denom,
    send_sem,
    recv_sem,
    local_sem,
):
    files, width = rows_hbm.shape
    devices = raw.shape[1]
    half = width // 2
    my_hx = lax.axis_index("hx")
    my_hy = lax.axis_index("hy")
    my_core = rem(my_hx, 2)
    my_y = div(my_hx, 2)
    my_x = div(my_hy, 4)
    my_z = rem(my_hy, 4)
    me = my_hx * 16 + my_hy

    def bucket_at(y, hy, name):
        offset = OFFSET[name]
        return 32 * y + 2 * rem(hy, 8) + offset + div(hy, 8) * (145 - 2 * offset)

    fetch_bucket = pltpu.make_async_copy(bucket_hbm, bucket_ref, local_sem.at[7])
    fetch_bucket.start()
    fetch = pltpu.make_async_copy(rows_hbm, rows_ref, local_sem.at[6])
    fetch.start()
    barrier = pltpu.get_barrier_semaphore()
    hxs = [rem(my_y + dy, 4) * 2 + rem(my_core + core, 2) for dy in range(4) for core in range(2)]
    hys = [rem(my_x + dx, 4) * 4 + rem(my_z + dz, 4) for dx in range(4) for dz in range(4)]
    far_first = sorted(
        ((row, column) for row in range(8) for column in range(16) if row or column),
        key=lambda at: -(apart(at[0] // 2) + apart(at[1] // 4) + apart(at[1] % 4)),
    )
    for row, column in far_first:
        pl.semaphore_signal(
            barrier, inc=1, device_id=(hxs[row], hys[column]), device_id_type=MESH
        )
    fetch_bucket.wait()

    bucket_f = bucket_ref[...].astype(jnp.float32)
    bucket_cols = jnp.broadcast_to(bucket_f, (128, files)).T
    rank = jnp.zeros((1, files), jnp.float32)
    lane = lax.broadcasted_iota(jnp.int32, (128, files), 1)
    sub = lax.broadcasted_iota(jnp.int32, (128, files), 0)
    for block in range(files // 128):
        col = bucket_cols[block * 128 : (block + 1) * 128, 0:1]
        same = (col == bucket_f) & (sub + block * 128 < lane)
        rank = rank + jnp.sum(jnp.where(same, 1.0, 0.0), axis=0, keepdims=True)
    target = bucket_f * float(SLOTS) + rank

    def mixed(one, two):
        low = lax.broadcasted_iota(jnp.int32, one.shape, 1) < SLOTS
        first = jnp.where(low, one, pltpu.roll(two, SLOTS, 1))
        second = jnp.where(low, pltpu.roll(one, SLOTS, 1), two)
        return first, second

    def fold_rows(values):
        count = values.shape[0] // 8
        one, two = mixed(
            values[:, :half].reshape(count, 8, half), values[:, half:].reshape(count, 8, half)
        )
        return jnp.stack([one, two], axis=1).reshape(count * 2, 8, half).astype(jnp.bfloat16)

    def unfold_rows(packed):
        count = packed.shape[0] // 2
        halves = packed.astype(jnp.float32).reshape(count, 2, 8, half)
        first, second = mixed(halves[:, 0], halves[:, 1])
        return first.reshape(count * 8, half), second.reshape(count * 8, half)

    fetch.wait()
    rows = rows_ref[...]

    def pack(block, carry):
        place = lax.broadcasted_iota(jnp.int32, (256, files), 0) + block * 256
        match = (place.astype(jnp.float32) == target).astype(jnp.float32)
        used = jnp.sum(match, axis=1, keepdims=True)
        packed = jnp.dot(match.astype(jnp.bfloat16), rows, preferred_element_type=jnp.float32)
        send_buf[pl.ds(block * 64, 64)] = fold_rows(jnp.where(used > 0.5, packed, EMPTY))
        return carry

    lax.fori_loop(0, BUCKETS * SLOTS // 256, pack, 0)

    pl.semaphore_wait(barrier, devices - 1)

    hy_low = [2 * rem(hy, 8) for hy in hys]
    hy_flip = [div(hy, 8) for hy in hys]
    cross = [(column // 4 + column) % 4 for column in range(16)]

    def send(y, column, core, slot):
        offset = OFFSET[DIRECT[core][slot]]
        pltpu.make_async_remote_copy(
            src_ref=send_buf.at[
                32 * y + hy_low[column] + offset + hy_flip[column] * (145 - 2 * offset)
            ],
            dst_ref=raw.at[slot, me],
            send_sem=send_sem.at[slot],
            recv_sem=recv_sem.at[slot],
            device_id=(y * 2 + core, hys[column]),
            device_id_type=MESH,
        ).start()

    def keep(core, slot):
        return pltpu.make_async_copy(
            send_buf.at[bucket_at(my_y, my_hy, DIRECT[core][slot])],
            raw.at[slot, me],
            local_sem.at[slot],
        )

    for core in range(2):

        @pl.when(my_core == core)
        def _():
            for slot in range(len(DIRECT[core])):
                keep(core, slot).start()
            for slot in range(len(DIRECT[1 - core])):
                send(my_y, 0, 1 - core, slot)

    def send_slot(slot, cores):
        def around(turn, carry):
            ys = [rem(my_y + turn + 2 * my_core + shift, 4) for shift in range(4)]
            for column in MIXED[1:]:
                for core in cores:
                    send(ys[cross[column]], column, core, slot)

            @pl.when(rem(turn + 2 * my_core, 4) > 0)
            def _():
                for core in cores:
                    send(ys[0], 0, core, slot)

            return carry

        lax.fori_loop(0, 4, around, 0)

    chips = devices // 2
    send_slot(0, (0, 1))
    send_slot(1, (0, 1))
    send_slot(2, (0, 1))
    send_slot(3, (1,))

    number = bucket_ref[...]
    high, mid, least = (number // place % 2 for place in (128, 16, 1))
    flip = (high + mid + least) // 2
    section = (
        3 * (high + flip - 2 * high * flip)
        + 2 * (mid + flip - 2 * mid * flip)
        + (least + flip - 2 * least * flip)
    )
    chip_of = number // 32 % 4 * 16 + flip * 8 + number // 2 % 8
    home_row = ((section * chips + chip_of) * SLOTS).astype(jnp.float32) + rank
    slot_cols = jnp.broadcast_to(home_row, (128, files)).T
    slot_wide = jnp.concatenate([slot_cols, slot_cols], axis=1)
    place = lax.broadcasted_iota(jnp.int32, (files, 256), 1).astype(jnp.float32)
    for block in range(4):
        match = (slot_wide == place + float(block * 256)).astype(jnp.float32)
        match_buf[block] = match.astype(jnp.bfloat16)

    def wait_count(buf, count, sem):
        part = buf.at[pl.ds(0, count)]
        pltpu.make_async_copy(part, part, sem).wait()

    def wait_slot(slot):
        wait_count(raw.at[slot], devices - 1, recv_sem.at[slot])

    def share(slot, there, sem):
        return pltpu.make_async_remote_copy(
            src_ref=raw.at[slot],
            dst_ref=raw.at[there],
            send_sem=send_sem.at[sem],
            recv_sem=recv_sem.at[there],
            device_id=(my_y * 2 + 1 - my_core, my_hy),
            device_id_type=MESH,
        )

    def wait_shared(slot):
        wait_count(raw.at[slot], devices, recv_sem.at[slot])

    scale_fold = sharpness / width * math.log2(math.e)

    def settle(slot, with_query):
        def block_step(block, carry):
            first, second = unfold_rows(raw[slot, pl.ds(block * SPAN, SPAN)])
            start = pl.multiple_of(block * (SPAN * 4), SPAN * 4)
            square = jnp.sum(first * first + second * second, axis=1, keepdims=True)
            inverse = 1.0 / jnp.sqrt(square * (1.0 / width) + epsilon)
            used = first[:, 0:1] < 100.0
            wide = jnp.broadcast_to(jnp.where(used, inverse, -1.0), (SPAN * 4, 128))
            across = wide.T[0:1, :]
            keys[slot, pl.ds(start, SPAN * 4), 0:half] = first.astype(jnp.bfloat16)
            keys[slot, pl.ds(start, SPAN * 4), half:width] = second.astype(jnp.bfloat16)
            key_scale[slot, :, pl.ds(start, SPAN * 4)] = across
            key_bias[slot, :, pl.ds(start, SPAN * 4)] = jnp.where(across > 0.0, 0.0, FAR)
            if with_query:
                query_scale[slot, pl.ds(start, SPAN * 4), :] = jnp.broadcast_to(
                    inverse * scale_fold, (SPAN * 4, 128)
                )
            return carry

        lax.fori_loop(0, devices // SPAN, block_step, 0)

    def pair_tile(query, start, tile, key, skip_self):
        queries = keys[query, pl.ds(start, tile), :]
        against = keys[key]
        products = lax.dot_general(
            queries, against, (((1,), (1,)), ((), ())), preferred_element_type=jnp.float32
        )
        scale = query_scale[query, pl.ds(start, tile), :][:, 0:1]
        weight = jnp.exp2(products * scale * key_scale[key] + key_bias[key])
        if skip_self:
            row = lax.broadcasted_iota(jnp.int32, (tile, CAP), 0) + start
            col = lax.broadcasted_iota(jnp.int32, (tile, CAP), 1)
            weight = jnp.where(row == col, 0.0, weight)
        total = weight[:, 0:128]
        for part in range(1, CAP // 128):
            total = total + weight[:, part * 128 : (part + 1) * 128]
        summed = jnp.dot(weight.astype(jnp.bfloat16), against, preferred_element_type=jnp.float32)
        return summed, total

    def own_pair(query):
        summed, total = pair_tile(query, 0, CAP, query, True)
        numer[query] = summed
        denom[query] = total

    def pair(query, key):
        summed, total = pair_tile(query, 0, CAP, key, False)
        numer[query] += summed
        denom[query] += total

    def keep_back(query):
        return pltpu.make_async_copy(
            back_buf.at[query, me],
            home_buf.at[2 * my_core + query, my_y * 16 + my_hy],
            local_sem.at[4 + query],
        )

    def finish(query, key):
        mine = 2 * my_core + query

        def block_step(step, carry):
            upper = rem(div(my_y, 2) + 1 + step, 2)
            start = pl.multiple_of(upper * 256, 256)
            summed, total = pair_tile(query, start, 256, key, False)
            whole = numer[query, pl.ds(start, 256), :] + summed
            under = denom[query, pl.ds(start, 256), :] + total
            under = 1.0 + jnp.sum(under, axis=1, keepdims=True)
            back_buf[query, pl.ds(upper * 64, 64)] = fold_rows(whole * (1.0 / under))

            def give(turn, inner):
                y = 2 * upper + rem(my_y + 1 + turn, 2)
                for column in MIXED[::-1]:
                    for core in range(2):
                        to = (y * 2 + core) * 16 + hys[column]

                        def start_copy():
                            pltpu.make_async_remote_copy(
                                src_ref=back_buf.at[query, to],
                                dst_ref=home_buf.at[mine, my_y * 16 + my_hy],
                                send_sem=send_sem.at[7 + query],
                                recv_sem=recv_sem.at[6 + mine],
                                device_id=(y * 2 + core, hys[column]),
                                device_id_type=MESH,
                            ).start()

                        if column:
                            start_copy()
                        else:
                            pl.when(to != me)(start_copy)
                return inner

            lax.fori_loop(0, 2, give, 0)
            return carry

        lax.fori_loop(0, 2, block_step, 0)
        keep_back(query).start()

    wait_slot(0)
    keep(0, 0).wait()
    first_share = share(0, 4 - my_core, 4)
    first_share.start()
    settle(0, True)
    own_pair(0)
    given = 3 + my_core
    wait_shared(given)
    settle(given, False)
    pair(0, given)
    wait_slot(1)
    keep(0, 1).wait()

    @pl.when(my_core == 1)
    def _():
        share(1, 4, 5).start()

    settle(1, True)

    @pl.when(my_core == 0)
    def _():
        pair(0, 1)
        wait_shared(4)
        settle(4, False)
        finish(0, 4)

    own_pair(1)
    pair(1, 4 * my_core)
    wait_slot(2)
    keep(0, 2).wait()
    second_share = share(2, 5, 6)
    second_share.start()
    settle(2, False)
    pair(1 - my_core, 2)
    wait_shared(5)
    settle(5, False)

    @pl.when(my_core == 1)
    def _():
        pair(1, 5)
        wait_slot(3)
        keep(1, 3).wait()
        settle(3, False)

    def last(index, carry):
        finish(1 - my_core + index, 5 - 2 * my_core)
        return carry

    lax.fori_loop(0, 1 + my_core, last, 0)
    keep_back(0).wait()
    keep_back(1).wait()
    first_share.wait_send()
    second_share.wait_send()

    @pl.when(my_core == 1)
    def _():
        share(1, 4, 5).wait_send()

    results = [0.0, 0.0]
    for block in range(4):
        for core in range(2):

            @pl.when(my_core == core)
            def _():
                count = chips - 1 if block // 2 == core else chips
                wait_count(home_buf.at[block], count, recv_sem.at[6 + block])

        parts = unfold_rows(home_buf[block])
        results = [
            result
            + jnp.dot(match_buf[block], part.astype(jnp.bfloat16), preferred_element_type=jnp.float32)
            for result, part in zip(results, parts)
        ]
    out_ref[:, 0:half] = results[0].astype(jnp.bfloat16)
    out_ref[:, half:width] = results[1].astype(jnp.bfloat16)

    for slot in range(3):
        wait_count(raw.at[slot], devices - 1, send_sem.at[slot])
    for core in range(2):

        @pl.when(my_core == core)
        def _():
            wait_count(raw.at[3], chips - core, send_sem.at[3])

    for query in range(2):
        wait_count(raw.at[query], devices - 1, send_sem.at[7 + query])


def solution(mesh):
    devices = mesh.shape["hx"] * mesh.shape["hy"]

    def body(embeddings, bucket):
        files, width = embeddings.shape
        half = width // 2
        return pl.pallas_call(
            kernel,
            out_shape=jax.ShapeDtypeStruct((files, width), jnp.bfloat16),
            in_specs=[pl.BlockSpec(memory_space=pltpu.HBM)] * 2,
            out_specs=pl.BlockSpec(memory_space=pltpu.VMEM),
            scratch_shapes=[
                pltpu.VMEM((files, width), jnp.bfloat16),
                pltpu.VMEM((1, files), jnp.int32),
                pltpu.VMEM((BUCKETS, 8, half), jnp.bfloat16),
                pltpu.VMEM((6, devices, 8, half), jnp.bfloat16),
                pltpu.VMEM((2, devices, 8, half), jnp.bfloat16),
                pltpu.VMEM((4, devices // 2, 8, half), jnp.bfloat16),
                pltpu.VMEM((4, files, 256), jnp.bfloat16),
                pltpu.VMEM((6, CAP, width), jnp.bfloat16),
                pltpu.VMEM((6, 1, CAP), jnp.float32),
                pltpu.VMEM((6, 1, CAP), jnp.float32),
                pltpu.VMEM((2, CAP, 128), jnp.float32),
                pltpu.VMEM((2, CAP, width), jnp.float32),
                pltpu.VMEM((2, CAP, 128), jnp.float32),
                pltpu.SemaphoreType.DMA((9,)),
                pltpu.SemaphoreType.DMA((10,)),
                pltpu.SemaphoreType.DMA((8,)),
            ],
            compiler_params=pltpu.CompilerParams(
                collective_id=0, has_side_effects=True, vmem_limit_bytes=32 * 1024 * 1024
            ),
        )(
            pltpu.with_memory_space_constraint(embeddings, pltpu.HBM),
            pltpu.with_memory_space_constraint(bucket.reshape(1, files), pltpu.HBM),
        )

    return jax.shard_map(
        body,
        mesh=mesh,
        in_specs=(P(("hx", "hy"), None), P(("hx", "hy"))),
        out_specs=P(("hx", "hy"), None),
        check_vma=False,
    )
```

```python
import functools
import math

import jax
import jax.numpy as jnp
from jax import lax
from jax.experimental import pallas as pl
from jax.experimental.pallas import tpu as pltpu
from jax.sharding import PartitionSpec as P

MESH = pl.DeviceIdType.MESH

CAP = 512
BUCKETS = 256
SLOTS = 4
sharpness = 32.0
epsilon = 1e-06
EMPTY = 128.0
FAR = -1e30
SPAN = 64
MIXED = [at % 4 * 4 + (at // 4 + at) % 4 for at in range(16)]

OFFSET = {name: 128 * (name // 100) + 16 * (name // 10 % 10) + name % 10 for name in (0, 1, 10, 11, 100, 101, 110)}
DIRECT = ((0, 1, 101), (10, 100, 11, 110))


def rem(value, by):
    return lax.rem(value, jnp.int32(by))


def div(value, by):
    return lax.div(value, jnp.int32(by))


def apart(shift):
    return min(shift, 4 - shift)


def kernel(
    rows_hbm,
    bucket_hbm,
    out_ref,
    rows_ref,
    bucket_ref,
    send_buf,
    raw,
    back_buf,
    home_buf,
    match_buf,
    keys,
    key_scale,
    key_bias,
    query_scale,
    numer,
    denom,
    send_sem,
    recv_sem,
    local_sem,
):
    files, width = rows_hbm.shape
    devices = raw.shape[1]
    half = width // 2
    my_hx = lax.axis_index("hx")
    my_hy = lax.axis_index("hy")
    my_core = rem(my_hx, 2)
    my_y = div(my_hx, 2)
    my_x = div(my_hy, 4)
    my_z = rem(my_hy, 4)
    me = my_hx * 16 + my_hy

    def bucket_at(y, hy, name):
        offset = OFFSET[name]
        return 32 * y + 2 * rem(hy, 8) + offset + div(hy, 8) * (145 - 2 * offset)

    fetch_bucket = pltpu.make_async_copy(bucket_hbm, bucket_ref, local_sem.at[7])
    fetch_bucket.start()
    fetch = pltpu.make_async_copy(rows_hbm, rows_ref, local_sem.at[6])
    fetch.start()
    barrier = pltpu.get_barrier_semaphore()
    hxs = [rem(my_y + dy, 4) * 2 + rem(my_core + core, 2) for dy in range(4) for core in range(2)]
    hys = [rem(my_x + dx, 4) * 4 + rem(my_z + dz, 4) for dx in range(4) for dz in range(4)]
    far_first = sorted(
        ((row, column) for row in range(8) for column in range(16) if row or column),
        key=lambda at: -(apart(at[0] // 2) + apart(at[1] // 4) + apart(at[1] % 4)),
    )
    for row, column in far_first:
        pl.semaphore_signal(
            barrier, inc=1, device_id=(hxs[row], hys[column]), device_id_type=MESH
        )
    fetch_bucket.wait()

    bucket_f = bucket_ref[...].astype(jnp.float32)
    bucket_cols = jnp.broadcast_to(bucket_f, (128, files)).T
    rank = jnp.zeros((1, files), jnp.float32)
    lane = lax.broadcasted_iota(jnp.int32, (128, files), 1)
    sub = lax.broadcasted_iota(jnp.int32, (128, files), 0)
    for block in range(files // 128):
        col = bucket_cols[block * 128 : (block + 1) * 128, 0:1]
        same = (col == bucket_f) & (sub + block * 128 < lane)
        rank = rank + jnp.sum(jnp.where(same, 1.0, 0.0), axis=0, keepdims=True)
    target = bucket_f * float(SLOTS) + rank

    def mixed(one, two):
        low = lax.broadcasted_iota(jnp.int32, one.shape, 1) < SLOTS
        first = jnp.where(low, one, pltpu.roll(two, SLOTS, 1))
        second = jnp.where(low, pltpu.roll(one, SLOTS, 1), two)
        return first, second

    def fold_rows(values):
        count = values.shape[0] // 8
        one, two = mixed(
            values[:, :half].reshape(count, 8, half), values[:, half:].reshape(count, 8, half)
        )
        return jnp.stack([one, two], axis=1).reshape(count * 2, 8, half).astype(jnp.bfloat16)

    def unfold_rows(packed):
        count = packed.shape[0] // 2
        halves = packed.astype(jnp.float32).reshape(count, 2, 8, half)
        first, second = mixed(halves[:, 0], halves[:, 1])
        return first.reshape(count * 8, half), second.reshape(count * 8, half)

    fetch.wait()
    rows = rows_ref[...]

    def pack(block, carry):
        place = lax.broadcasted_iota(jnp.int32, (256, files), 0) + block * 256
        match = (place.astype(jnp.float32) == target).astype(jnp.float32)
        used = jnp.sum(match, axis=1, keepdims=True)
        packed = jnp.dot(match.astype(jnp.bfloat16), rows, preferred_element_type=jnp.float32)
        send_buf[pl.ds(block * 64, 64)] = fold_rows(jnp.where(used > 0.5, packed, EMPTY))
        return carry

    lax.fori_loop(0, BUCKETS * SLOTS // 256, pack, 0)

    pl.semaphore_wait(barrier, devices - 1)

    hy_low = [2 * rem(hy, 8) for hy in hys]
    hy_flip = [div(hy, 8) for hy in hys]
    cross = [(column // 4 + column) % 4 for column in range(16)]

    def send(y, column, core, slot):
        offset = OFFSET[DIRECT[core][slot]]
        pltpu.make_async_remote_copy(
            src_ref=send_buf.at[
                32 * y + hy_low[column] + offset + hy_flip[column] * (145 - 2 * offset)
            ],
            dst_ref=raw.at[slot, me],
            send_sem=send_sem.at[slot],
            recv_sem=recv_sem.at[slot],
            device_id=(y * 2 + core, hys[column]),
            device_id_type=MESH,
        ).start()

    def keep(core, slot):
        return pltpu.make_async_copy(
            send_buf.at[bucket_at(my_y, my_hy, DIRECT[core][slot])],
            raw.at[slot, me],
            local_sem.at[slot],
        )

    for core in range(2):

        @pl.when(my_core == core)
        def _():
            for slot in range(len(DIRECT[core])):
                keep(core, slot).start()
            for slot in range(len(DIRECT[1 - core])):
                send(my_y, 0, 1 - core, slot)

    def send_slot(slot, cores):
        def around(turn, carry):
            ys = [rem(my_y + turn + 2 * my_core + shift, 4) for shift in range(4)]
            for column in MIXED[1:]:
                for core in cores:
                    send(ys[cross[column]], column, core, slot)

            @pl.when(rem(turn + 2 * my_core, 4) > 0)
            def _():
                for core in cores:
                    send(ys[0], 0, core, slot)

            return carry

        lax.fori_loop(0, 4, around, 0)

    chips = devices // 2
    send_slot(0, (0, 1))
    send_slot(1, (0, 1))
    send_slot(2, (0, 1))
    send_slot(3, (1,))

    number = bucket_ref[...]
    high, mid, least = (number // place % 2 for place in (128, 16, 1))
    flip = (high + mid + least) // 2
    section = (
        3 * (high + flip - 2 * high * flip)
        + 2 * (mid + flip - 2 * mid * flip)
        + (least + flip - 2 * least * flip)
    )
    chip_of = number // 32 % 4 * 16 + flip * 8 + number // 2 % 8
    home_row = ((section * chips + chip_of) * SLOTS).astype(jnp.float32) + rank
    slot_cols = jnp.broadcast_to(home_row, (128, files)).T
    slot_wide = jnp.concatenate([slot_cols, slot_cols], axis=1)
    place = lax.broadcasted_iota(jnp.int32, (files, 256), 1).astype(jnp.float32)
    for block in range(4):
        match = (slot_wide == place + float(block * 256)).astype(jnp.float32)
        match_buf[block] = match.astype(jnp.bfloat16)

    def wait_count(buf, count, sem):
        part = buf.at[pl.ds(0, count)]
        pltpu.make_async_copy(part, part, sem).wait()

    def wait_slot(slot):
        wait_count(raw.at[slot], devices - 1, recv_sem.at[slot])

    def share(slot, there, sem):
        return pltpu.make_async_remote_copy(
            src_ref=raw.at[slot],
            dst_ref=raw.at[there],
            send_sem=send_sem.at[sem],
            recv_sem=recv_sem.at[there],
            device_id=(my_y * 2 + 1 - my_core, my_hy),
            device_id_type=MESH,
        )

    def wait_shared(slot):
        wait_count(raw.at[slot], devices, recv_sem.at[slot])

    scale_fold = sharpness / width * math.log2(math.e)

    def settle(slot, with_query):
        def block_step(block, carry):
            first, second = unfold_rows(raw[slot, pl.ds(block * SPAN, SPAN)])
            start = pl.multiple_of(block * (SPAN * 4), SPAN * 4)
            square = jnp.sum(first * first + second * second, axis=1, keepdims=True)
            inverse = 1.0 / jnp.sqrt(square * (1.0 / width) + epsilon)
            used = first[:, 0:1] < 100.0
            wide = jnp.broadcast_to(jnp.where(used, inverse, -1.0), (SPAN * 4, 128))
            across = wide.T[0:1, :]
            keys[slot, pl.ds(start, SPAN * 4), 0:half] = first.astype(jnp.bfloat16)
            keys[slot, pl.ds(start, SPAN * 4), half:width] = second.astype(jnp.bfloat16)
            key_scale[slot, :, pl.ds(start, SPAN * 4)] = across
            key_bias[slot, :, pl.ds(start, SPAN * 4)] = jnp.where(across > 0.0, 0.0, FAR)
            if with_query:
                query_scale[slot, pl.ds(start, SPAN * 4), :] = jnp.broadcast_to(
                    inverse * scale_fold, (SPAN * 4, 128)
                )
            return carry

        lax.fori_loop(0, devices // SPAN, block_step, 0)

    def pair_tile(query, start, tile, key, skip_self):
        queries = keys[query, pl.ds(start, tile), :]
        against = keys[key]
        products = lax.dot_general(
            queries, against, (((1,), (1,)), ((), ())), preferred_element_type=jnp.float32
        )
        scale = query_scale[query, pl.ds(start, tile), :][:, 0:1]
        weight = jnp.exp2(products * scale * key_scale[key] + key_bias[key])
        if skip_self:
            row = lax.broadcasted_iota(jnp.int32, (tile, CAP), 0) + start
            col = lax.broadcasted_iota(jnp.int32, (tile, CAP), 1)
            weight = jnp.where(row == col, 0.0, weight)
        total = weight[:, 0:128]
        for part in range(1, CAP // 128):
            total = total + weight[:, part * 128 : (part + 1) * 128]
        summed = jnp.dot(weight.astype(jnp.bfloat16), against, preferred_element_type=jnp.float32)
        return summed, total

    def own_pair(query):
        summed, total = pair_tile(query, 0, CAP, query, True)
        numer[query] = summed
        denom[query] = total

    def pair(query, key):
        summed, total = pair_tile(query, 0, CAP, key, False)
        numer[query] += summed
        denom[query] += total

    def keep_back(query):
        return pltpu.make_async_copy(
            back_buf.at[query, me],
            home_buf.at[2 * my_core + query, my_y * 16 + my_hy],
            local_sem.at[4 + query],
        )

    def finish(query, key):
        mine = 2 * my_core + query

        def block_step(step, carry):
            upper = rem(div(my_y, 2) + 1 + step, 2)
            start = pl.multiple_of(upper * 256, 256)
            summed, total = pair_tile(query, start, 256, key, False)
            whole = numer[query, pl.ds(start, 256), :] + summed
            under = denom[query, pl.ds(start, 256), :] + total
            under = 1.0 + jnp.sum(under, axis=1, keepdims=True)
            back_buf[query, pl.ds(upper * 64, 64)] = fold_rows(whole * (1.0 / under))

            def give(turn, inner):
                y = 2 * upper + rem(my_y + 1 + turn + my_core, 2)
                for column in MIXED[::-1]:
                    for core in range(2):
                        to = (y * 2 + core) * 16 + hys[column]

                        def start_copy():
                            pltpu.make_async_remote_copy(
                                src_ref=back_buf.at[query, to],
                                dst_ref=home_buf.at[mine, my_y * 16 + my_hy],
                                send_sem=send_sem.at[7 + query],
                                recv_sem=recv_sem.at[6 + mine],
                                device_id=(y * 2 + core, hys[column]),
                                device_id_type=MESH,
                            ).start()

                        if column:
                            start_copy()
                        else:
                            pl.when(to != me)(start_copy)
                return inner

            lax.fori_loop(0, 2, give, 0)
            return carry

        lax.fori_loop(0, 2, block_step, 0)
        keep_back(query).start()

    wait_slot(0)
    keep(0, 0).wait()
    first_share = share(0, 4 - my_core, 4)
    first_share.start()
    settle(0, True)
    own_pair(0)
    given = 3 + my_core
    wait_shared(given)
    settle(given, False)
    pair(0, given)
    wait_slot(1)
    keep(0, 1).wait()

    @pl.when(my_core == 1)
    def _():
        share(1, 4, 5).start()

    settle(1, True)

    @pl.when(my_core == 0)
    def _():
        pair(0, 1)
        wait_shared(4)
        settle(4, False)
        finish(0, 4)

    own_pair(1)
    pair(1, 4 * my_core)
    wait_slot(2)
    keep(0, 2).wait()
    second_share = share(2, 5, 6)
    second_share.start()
    settle(2, False)
    pair(1 - my_core, 2)
    wait_shared(5)
    settle(5, False)

    @pl.when(my_core == 1)
    def _():
        pair(1, 5)
        wait_slot(3)
        keep(1, 3).wait()
        settle(3, False)

    def last(index, carry):
        finish(1 - my_core + index, 5 - 2 * my_core)
        return carry

    lax.fori_loop(0, 1 + my_core, last, 0)
    keep_back(0).wait()
    keep_back(1).wait()
    first_share.wait_send()
    second_share.wait_send()

    @pl.when(my_core == 1)
    def _():
        share(1, 4, 5).wait_send()

    results = [0.0, 0.0]
    for block in range(4):
        for core in range(2):

            @pl.when(my_core == core)
            def _():
                count = chips - 1 if block // 2 == core else chips
                wait_count(home_buf.at[block], count, recv_sem.at[6 + block])

        parts = unfold_rows(home_buf[block])
        results = [
            result
            + jnp.dot(match_buf[block], part.astype(jnp.bfloat16), preferred_element_type=jnp.float32)
            for result, part in zip(results, parts)
        ]
    out_ref[:, 0:half] = results[0].astype(jnp.bfloat16)
    out_ref[:, half:width] = results[1].astype(jnp.bfloat16)

    for slot in range(3):
        wait_count(raw.at[slot], devices - 1, send_sem.at[slot])
    for core in range(2):

        @pl.when(my_core == core)
        def _():
            wait_count(raw.at[3], chips - core, send_sem.at[3])

    for query in range(2):
        wait_count(raw.at[query], devices - 1, send_sem.at[7 + query])


def solution(mesh):
    devices = mesh.shape["hx"] * mesh.shape["hy"]

    def body(embeddings, bucket):
        files, width = embeddings.shape
        half = width // 2
        return pl.pallas_call(
            kernel,
            out_shape=jax.ShapeDtypeStruct((files, width), jnp.bfloat16),
            in_specs=[pl.BlockSpec(memory_space=pltpu.HBM)] * 2,
            out_specs=pl.BlockSpec(memory_space=pltpu.VMEM),
            scratch_shapes=[
                pltpu.VMEM((files, width), jnp.bfloat16),
                pltpu.VMEM((1, files), jnp.int32),
                pltpu.VMEM((BUCKETS, 8, half), jnp.bfloat16),
                pltpu.VMEM((6, devices, 8, half), jnp.bfloat16),
                pltpu.VMEM((2, devices, 8, half), jnp.bfloat16),
                pltpu.VMEM((4, devices // 2, 8, half), jnp.bfloat16),
                pltpu.VMEM((4, files, 256), jnp.bfloat16),
                pltpu.VMEM((6, CAP, width), jnp.bfloat16),
                pltpu.VMEM((6, 1, CAP), jnp.float32),
                pltpu.VMEM((6, 1, CAP), jnp.float32),
                pltpu.VMEM((2, CAP, 128), jnp.float32),
                pltpu.VMEM((2, CAP, width), jnp.float32),
                pltpu.VMEM((2, CAP, 128), jnp.float32),
                pltpu.SemaphoreType.DMA((9,)),
                pltpu.SemaphoreType.DMA((10,)),
                pltpu.SemaphoreType.DMA((8,)),
            ],
            compiler_params=pltpu.CompilerParams(
                collective_id=0, has_side_effects=True, vmem_limit_bytes=32 * 1024 * 1024
            ),
        )(
            pltpu.with_memory_space_constraint(embeddings, pltpu.HBM),
            pltpu.with_memory_space_constraint(bucket.reshape(1, files), pltpu.HBM),
        )

    return jax.shard_map(
        body,
        mesh=mesh,
        in_specs=(P(("hx", "hy"), None), P(("hx", "hy"))),
        out_specs=P(("hx", "hy"), None),
        check_vma=False,
    )
```
